256 devices in a mesh: rows: 32 (over x, z), cols: 8 (over y, core).
Axes of the slice: x: 4, y: 4, z: 8, core: 2. Of those that a mesh axis runs over, the one named last changes fastest.
Arguments:
- hankel: float32 [1024, 32768], P('rows', 'cols'), may hold values from -6 to 6
- shifted: float32 [1024, 32768], P('rows', 'cols'), may hold values from -6 to 6
- start_basis: float32 [32768, 128], P(('cols', 'rows')), may hold values from -0.03125 to 0.03125
Outputs:
- basis: float32 [1024, 128], P('rows')
- operator: float32 [128, 128], replicated
The draws below stay inside these ranges and needn't reach their ends.
All inputs are finite; a program needn't handle non-finite values.
Results may differ from the reference program's by a relative error of at most 0.0002.
Values sent between devices are 32-bit elements; how exact they have to be, the bound alone decides.
No kernel may reach another device: no remote copies, remote signals or barrier semaphores. Data moves between devices by JAX's collectives and lax.ppermute only.
A program may use at most 64 MiB of HBM per device.

```python
import math
import jax
import jax.numpy as jnp
from jax import lax

S = 32768
K = 128
P_SIZE = 1024


def with_spikes(drawn, key, source, target, blocks, factor):
    owner, partner = [(jnp.arange(drawn.shape[dim]) // (drawn.shape[dim] // blocks)).reshape([-1 if axis == dim else 1 for axis in range(drawn.ndim)]) for dim in (source, target)]
    chosen = jax.random.permutation(key, blocks)[partner]
    strong = (owner == chosen) | (owner == (partner + blocks // 2) % blocks)
    return jnp.where(strong, factor * drawn, drawn)


def level_of(stream_key, dims, cuts, low, high):
    def one(dim, shards_of):
        draws = jax.random.uniform(jax.random.fold_in(jax.random.fold_in(stream_key, 6), dim), (shards_of,), jnp.float32, low / len(cuts), high / len(cuts))
        return jnp.repeat(jnp.exp(draws), dims[dim] // shards_of).reshape((-1,) + (1,) * (len(dims) - dim - 1))

    factor_of = one(*cuts[0])
    for cut in cuts[1:]:
        factor_of = factor_of * one(*cut)
    return factor_of


def centred(key, shape, spread, reach, shards=(), kind=jnp.bfloat16):
    array = jax.random.normal(key, shape, jnp.float32) * spread
    if len(shards) > 0:
        array = level_of(key, shape, shards, -0.22, 0.18) * array
    return jnp.clip(array, min=-reach, max=reach).astype(kind)


def gaussian_with(rng, extent, spread, bound, shards, heavy, dtype=jnp.bfloat16):
    drawn = spread * jax.random.normal(rng, extent, jnp.float32)
    if shards:
        drawn = drawn * level_of(rng, extent, shards, -0.22, 0.18)
    return jnp.clip(with_spikes(drawn, jax.random.fold_in(rng, 3), *heavy), -bound, bound).astype(dtype)


def setup_inputs(seed: int = 0) -> dict:
    arg_keys = jax.random.split(jax.random.key(seed), 4)
    hankel = gaussian_with(arg_keys[0], (P_SIZE, S), 1.0, 6.0, ((0, 32), (1, 8)), (0, 1, 32, 2.75), jnp.float32)
    shifted = centred(arg_keys[1], (P_SIZE, S), 1.0, 6.0, ((0, 32), (1, 8)), jnp.float32)
    start_basis = centred(arg_keys[2], (S, K), S ** -0.5, 0.03125, ((0, 256),), jnp.float32)
    return {"hankel": hankel, "shifted": shifted, "start_basis": start_basis}


def product(left, right):
    return jnp.dot(left.astype(jnp.float32), right.astype(jnp.float32), precision=lax.Precision.HIGHEST, preferred_element_type=jnp.float32)

def right_solve(values, lower):
    return lax.linalg.triangular_solve(lower, values, left_side=False, lower=True, transpose_a=True)

def orthonormal(columns, total):
    gram = product(columns.T, columns) / total
    lower = jnp.linalg.cholesky(gram)
    return right_solve(columns, lower)

def reference(hankel, shifted, start_basis):
    total = hankel.shape[0]
    columns = product(hankel, start_basis)
    left = orthonormal(columns, total)
    across = product(hankel.T, left)
    lower_w = jnp.linalg.cholesky(product(across.T, across))
    right = right_solve(across, lower_w)
    columns = product(hankel, right)
    image = product(shifted, right)
    basis = orthonormal(columns, total)
    operator = product(basis.T, image) * (1.0 / math.sqrt(total))
    return (basis, operator)
```

```python
import jax
import jax.numpy as jnp
from jax import lax
from jax.sharding import Mesh
from jax.sharding import PartitionSpec as P

ROWS = ("x", "z")
COLS = ("y", "core")
CHIPS = ("x", "z", "y")
CHANGE = ("x", "z", "core")


def einsum(spec, left, right):
    return jnp.einsum(
        spec, left, right, precision=lax.Precision.HIGHEST, preferred_element_type=jnp.float32
    )


def exchanged(blocks, axis):
    return lax.all_to_all(blocks, axis, 0, 0, tiled=True)


def from_other_core(value):
    return lax.ppermute(value, "core", [(0, 1), (1, 0)])


def by_suffix(block):
    rows, cols = block.shape
    groups = lax.axis_size(ROWS)
    pieces = block.reshape(2, rows // 2, groups, cols // groups).transpose(2, 0, 1, 3)
    pieces = pieces.reshape(2 * groups, rows // 2, cols // groups)
    return exchanged(pieces, CHANGE).reshape(groups, 2, rows // 2, cols // groups)


def summed_over_chips(part):
    chips = lax.axis_size(CHIPS)
    mine = jnp.sum(exchanged(part.reshape(chips, -1, part.shape[-1]), CHIPS), axis=0)
    copies = jnp.broadcast_to(mine[None], (chips, *mine.shape))
    return exchanged(copies, CHIPS).reshape(part.shape)


def inverse_or_zero(scale):
    return jnp.where(scale > 0, 1.0 / jnp.where(scale > 0, scale, 1.0), 0.0)


def on_device(hankel, shifted, start_basis):
    rows_dev, _ = hankel.shape
    rank = start_basis.shape[1]
    core = lax.axis_index("core")
    other_start = from_other_core(start_basis)
    h = by_suffix(hankel)
    t = by_suffix(shifted)
    start = jnp.where(
        core == 0, jnp.stack([start_basis, other_start]), jnp.stack([other_start, start_basis])
    )
    groups, _, half, _ = h.shape
    c_part = einsum("rkij,kjn->rin", h, start).reshape(groups * half, rank)
    c = summed_over_chips(c_part)
    c_scale = jnp.max(jnp.abs(c))
    c = c * inverse_or_zero(c_scale)
    x_part = einsum("rkij,rin->kjn", h, c.reshape(groups, half, rank))
    x_other, c_scale_other = from_other_core(x_part), from_other_core(c_scale)
    c_largest = inverse_or_zero(jnp.maximum(c_scale, c_scale_other))
    x = x_part * (c_scale * c_largest) + x_other * (c_scale_other * c_largest)
    c = c * (c_scale * c_largest)
    y_part = einsum("rkij,kjn->rin", h, x).reshape(groups * half, rank)
    z_part = einsum("rkij,kjn->rin", t, x).reshape(groups * half, rank)
    yz = summed_over_chips(jnp.concatenate([y_part, z_part], axis=0))
    y, z = yz[: groups * half], yz[groups * half :]
    y_scale = jnp.max(jnp.abs(y))
    y = y * inverse_or_zero(y_scale)
    grams = einsum("pm,qpn->qmn", y, jnp.stack([y, z, c]))
    mine = lax.dynamic_slice_in_dim(y, lax.axis_index(ROWS) * half, half, 0)
    grams_other, mine_other, y_scale_other = (
        from_other_core(grams), from_other_core(mine), from_other_core(y_scale)
    )
    y_top = jnp.maximum(y_scale, y_scale_other)
    y_largest = inverse_or_zero(y_top)
    f, f_other = y_scale * y_largest, y_scale_other * y_largest
    gram = grams[0] * (f * f) + grams_other[0] * (f_other * f_other)
    cross = grams[1] * f + grams_other[1] * f_other
    gram_w = grams[2] * f + grams_other[2] * f_other
    lower = jnp.linalg.cholesky(gram)
    lower_w = jnp.linalg.cholesky(gram_w)
    mine, mine_other = mine * f, mine_other * f_other
    y_rows = jnp.where(
        core == 0, jnp.concatenate([mine, mine_other]), jnp.concatenate([mine_other, mine])
    )
    total = rows_dev * groups
    basis = lax.linalg.triangular_solve(
        lower, y_rows * jnp.sqrt(float(total)), left_side=False, lower=True, transpose_a=True
    )
    operator = lax.linalg.triangular_solve(lower, cross, left_side=True, lower=True)
    operator = lax.linalg.triangular_solve(
        lower_w, operator, left_side=False, lower=True, transpose_a=True
    )
    return basis, operator * lax.rsqrt(y_top)


def solution(mesh):
    finer = Mesh(mesh.devices.reshape(4, 8, 4, 2), ("x", "z", "y", "core"))
    placed = (P(ROWS, COLS), P(ROWS, COLS), P((*COLS, *ROWS), None))
    return jax.shard_map(
        on_device, mesh=finer, in_specs=placed, out_specs=(P(ROWS, None), P()), check_vma=False
    )
```

```python
import functools

import jax
import jax.numpy as jnp
from jax import lax
from jax.experimental import pallas as pl
from jax.experimental.pallas import tpu as pltpu
from jax.sharding import Mesh
from jax.sharding import PartitionSpec as P

ROWS = ("x", "z")
COLS = ("y", "core")
CHIPS = ("x", "z", "y")
CHANGE = ("x", "z", "core")
SUB, LANE = 8, 128


def exchanged(blocks, axis):
    return lax.all_to_all(blocks, axis, 0, 0, tiled=True)


def from_other_core(value):
    return lax.ppermute(value, "core", [(0, 1), (1, 0)])


def call(kernel, name, shapes, scalars, arrays):
    return pl.pallas_call(
        kernel,
        name=name,
        out_shape=[jax.ShapeDtypeStruct(shape, jnp.float32) for shape in shapes],
        in_specs=[pl.BlockSpec(memory_space=pltpu.SMEM)] * len(scalars)
        + [pl.BlockSpec(memory_space=pltpu.VMEM)] * len(arrays),
        out_specs=[pl.BlockSpec(memory_space=pltpu.VMEM)] * len(shapes),
        compiler_params=pltpu.CompilerParams(vmem_limit_bytes=24 << 20),
    )(*scalars, *arrays)


def dot(left, right, left_dim=1, right_dim=0):
    return lax.dot_general(
        left,
        right,
        (((left_dim,), (right_dim,)), ((), ())),
        precision=lax.Precision.HIGHEST,
        preferred_element_type=jnp.float32,
    )


def inverse_or_zero(scale):
    return jnp.where(scale > 0, 1.0 / jnp.where(scale > 0, scale, 1.0), 0.0)


def largest(value):
    return jnp.max(jnp.max(jnp.abs(value), axis=0, keepdims=True), axis=1, keepdims=True)


def split_kernel(h_ref, t_ref, out_ref):
    groups, _, half2, lanes = out_ref.shape
    half = half2 // 2
    for at, ref in ((0, h_ref), (half, t_ref)):
        for g in range(groups):
            for part in range(2):
                out_ref[g, part, at : at + half, :] = ref[
                    part * half : (part + 1) * half, g * lanes : (g + 1) * lanes
                ]


def block_of(ht_ref, part, which):
    groups, _, half2, lanes = ht_ref.shape
    half = half2 // 2
    block = ht_ref[:, part, which * half : (which + 1) * half, :]
    return block.reshape(groups * half, lanes)


def columns_kernel(core_ref, ht_ref, own_ref, other_ref, out_ref):
    first = core_ref[0] == 0
    own, other = own_ref[...], other_ref[...]
    out_ref[...] = dot(block_of(ht_ref, 0, 0), jnp.where(first, own, other)) + dot(
        block_of(ht_ref, 1, 0), jnp.where(first, other, own)
    )


def sum_kernel(in_ref, out_ref, *, rows):
    tiles = [in_ref[SUB * i : SUB * (i + 1), :] for i in range(in_ref.shape[0] // SUB)]
    while len(tiles) > 1:
        tiles = [a + b for a, b in zip(tiles[::2], tiles[1::2])]
    total = tiles[0]
    if rows < SUB:
        total = total + pltpu.roll(total, rows, 0)
    for i in range(out_ref.shape[0] // SUB):
        out_ref[SUB * i : SUB * (i + 1), :] = total


def across_kernel(ht_ref, c_ref, out_ref):
    c = c_ref[...]
    scale = largest(c)
    c = c * inverse_or_zero(scale)
    for part in range(2):
        out_ref[part * LANE : (part + 1) * LANE, :] = dot(block_of(ht_ref, part, 0), c, 0, 0)
    out_ref[2 * LANE :, :] = jnp.broadcast_to(scale, (SUB, LANE))


def image_kernel(ht_ref, own_ref, other_ref, out_ref):
    scale, scale_other = own_ref[2 * LANE : 2 * LANE + 1, :], other_ref[2 * LANE : 2 * LANE + 1, :]
    top = inverse_or_zero(jnp.maximum(scale, scale_other))
    x = own_ref[: 2 * LANE, :] * (scale * top) + other_ref[: 2 * LANE, :] * (scale_other * top)
    rows = out_ref.shape[0] // 2
    for which in range(2):
        out_ref[which * rows : (which + 1) * rows, :] = dot(
            block_of(ht_ref, 0, which), x[:LANE]
        ) + dot(block_of(ht_ref, 1, which), x[LANE:])


def gram_kernel(at_ref, yz_ref, c_ref, own_ref, other_ref, out_ref, *, half):
    scale, scale_other = own_ref[2 * LANE : 2 * LANE + 1, :], other_ref[2 * LANE : 2 * LANE + 1, :]
    top = inverse_or_zero(jnp.maximum(scale, scale_other))
    c = c_ref[...]
    c = c * (inverse_or_zero(scale) * (scale * top))
    rows = yz_ref.shape[0] // 2
    y = yz_ref[:rows, :]
    y_scale = largest(y)
    back = inverse_or_zero(y_scale)
    y = y * back
    out_ref[:LANE, :] = dot(y, y, 0, 0)
    out_ref[LANE : 2 * LANE, :] = dot(y, yz_ref[rows:, :], 0, 0)
    out_ref[2 * LANE : 3 * LANE, :] = dot(c, y, 0, 0)
    start = pl.multiple_of(at_ref[0] * half, half)
    out_ref[3 * LANE : 3 * LANE + half, :] = yz_ref[pl.ds(start, half), :] * back
    out_ref[3 * LANE + half :, :] = jnp.broadcast_to(y_scale, (SUB, LANE))


def inverse_factors(matrices):
    size = matrices[0].shape[0]
    blocks = size // SUB
    lane = lax.broadcasted_iota(jnp.int32, (SUB, size), 1)
    sub = lax.broadcasted_iota(jnp.int32, (SUB, size), 0)
    work = [[m[SUB * i : SUB * (i + 1), :] for i in range(blocks)] for m in matrices]

    def columns(rows, low):
        return [
            jnp.broadcast_to(rows[:, low + j : low + j + 1], (SUB, size)) for j in range(SUB)
        ]

    def row(values, j):
        return jnp.broadcast_to(values[j : j + 1, :], (SUB, size))

    for k in range(blocks):
        low = SUB * k
        inside = (lane >= low) & (lane < low + SUB)
        done = []
        for mine in work:
            column = columns(mine[k], low)
            w = jnp.where(inside, (lane == sub + low).astype(jnp.float32), mine[k])
            steps, pivots = [], jnp.ones((SUB, size), jnp.float32)
            for j in range(SUB):
                pivot = row(column[j], j)
                inverse = 1.0 / pivot
                pivots = jnp.where(sub == j, pivot, pivots)
                factor = jnp.where(sub > j, column[j] * inverse, 0.0)
                ahead = {}
                for i in range(j + 1, SUB):
                    ahead[i] = row(column[i], j)
                    column[i] = column[i] - factor * ahead[i]
                reduced = row(w, j)
                w = w - factor * reduced
                steps.append((inverse, ahead, reduced))
            root = lax.rsqrt(pivots)
            root = root * (1.5 - 0.5 * pivots * root * root)
            mine[k] = jnp.where(lane <= sub + low, w * root, 0.0)
            done.append(steps)
        for mine, steps in zip(work, done):
            for i in range(k + 1, blocks):
                column = columns(mine[i], low)
                w = jnp.where(inside, 0.0, mine[i])
                for j, (inverse, ahead, reduced) in enumerate(steps):
                    factor = column[j] * inverse
                    for n in range(j + 1, SUB):
                        column[n] = column[n] - factor * ahead[n]
                    w = w - factor * reduced
                mine[i] = w
    return [jnp.concatenate(mine, axis=0) for mine in work]


def final_kernel(core_ref, own_ref, other_ref, basis_ref, operator_ref, *, half, total):
    at = 3 * LANE + half
    scale, scale_other = own_ref[at : at + 1, :], other_ref[at : at + 1, :]
    top = jnp.maximum(scale, scale_other)
    back = inverse_or_zero(top)
    f, f_other = scale * back, scale_other * back
    gram = own_ref[:LANE, :] * (f * f) + other_ref[:LANE, :] * (f_other * f_other)
    cross = own_ref[LANE : 2 * LANE, :] * f + other_ref[LANE : 2 * LANE, :] * f_other
    gram_w = own_ref[2 * LANE : 3 * LANE, :] * f + other_ref[2 * LANE : 3 * LANE, :] * f_other
    lower, lower_w = inverse_factors([gram, gram_w])
    root = jnp.sqrt(jnp.float32(total))
    core = core_ref[0]
    for ref, factor, place in ((own_ref, f, core), (other_ref, f_other, 1 - core)):
        rows = ref[3 * LANE : at, :] * (factor * root)
        basis_ref[pl.ds(pl.multiple_of(place * half, half), half), :] = dot(rows, lower, 1, 1)
    operator_ref[...] = dot(dot(lower, cross), lower_w, 1, 1) * lax.rsqrt(top)


def summed_over_chips(part):
    chips = lax.axis_size(CHIPS)
    rows = part.shape[0] // chips
    blocks = exchanged(part.reshape(chips, rows, LANE), CHIPS).reshape(part.shape)
    (copies,) = call(
        functools.partial(sum_kernel, rows=rows), f"sum_{rows}", [part.shape], [], [blocks]
    )
    return exchanged(copies.reshape(chips, rows, LANE), CHIPS).reshape(part.shape)


def on_device(hankel, shifted, start_basis):
    rows_dev = hankel.shape[0]
    groups, half = lax.axis_size(ROWS), rows_dev // 2
    rows = groups * half
    core = lax.axis_index("core").astype(jnp.int32).reshape(1)
    place = lax.axis_index(ROWS).astype(jnp.int32).reshape(1)
    other_start = from_other_core(start_basis)
    (pieces,) = call(split_kernel, "split", [(groups, 2, rows_dev, LANE)], [], [hankel, shifted])
    pieces = exchanged(pieces.reshape(2 * groups, rows_dev, LANE), CHANGE)
    ht = pieces.reshape(groups, 2, rows_dev, LANE)
    (c_part,) = call(
        columns_kernel, "columns", [(rows, LANE)], [core], [ht, start_basis, other_start]
    )
    c = summed_over_chips(c_part)
    (x_part,) = call(across_kernel, "across", [(2 * LANE + SUB, LANE)], [], [ht, c])
    x_other = from_other_core(x_part)
    (yz_part,) = call(image_kernel, "image", [(2 * rows, LANE)], [], [ht, x_part, x_other])
    yz = summed_over_chips(yz_part)
    (grams,) = call(
        functools.partial(gram_kernel, half=half),
        "grams",
        [(3 * LANE + half + SUB, LANE)],
        [place],
        [yz, c, x_part, x_other],
    )
    return call(
        functools.partial(final_kernel, half=half, total=rows_dev * groups),
        "factors",
        [(rows_dev, LANE), (LANE, LANE)],
        [core],
        [grams, from_other_core(grams)],
    )


def solution(mesh):
    finer = Mesh(mesh.devices.reshape(4, 8, 4, 2), ("x", "z", "y", "core"))
    placed = (P(ROWS, COLS), P(ROWS, COLS), P((*COLS, *ROWS), None))

    def whole(*blocks):
        return tuple(on_device(*blocks))

    return jax.shard_map(
        whole, mesh=finer, in_specs=placed, out_specs=(P(ROWS, None), P()), check_vma=False
    )
```

```python
import functools

import jax
import jax.numpy as jnp
from jax import lax
from jax.experimental import pallas as pl
from jax.experimental.pallas import tpu as pltpu
from jax.sharding import Mesh
from jax.sharding import PartitionSpec as P

ROWS = ("x", "z")
COLS = ("y", "core")
PLANE = ("x", "y")
CHANGE = ("x", "z", "core")
SUB, LANE = 8, 128


def exchanged(blocks, axis):
    return lax.all_to_all(blocks, axis, 0, 0, tiled=True)


def from_other_core(value):
    return lax.ppermute(value, "core", [(0, 1), (1, 0)])


def call(kernel, name, shapes, scalars, arrays):
    return pl.pallas_call(
        kernel,
        name=name,
        out_shape=[jax.ShapeDtypeStruct(shape, jnp.float32) for shape in shapes],
        in_specs=[pl.BlockSpec(memory_space=pltpu.SMEM)] * len(scalars)
        + [pl.BlockSpec(memory_space=pltpu.VMEM)] * len(arrays),
        out_specs=[pl.BlockSpec(memory_space=pltpu.VMEM)] * len(shapes),
        compiler_params=pltpu.CompilerParams(vmem_limit_bytes=24 << 20),
    )(*scalars, *arrays)


def dot(left, right, left_dim=1, right_dim=0):
    return lax.dot_general(
        left,
        right,
        (((left_dim,), (right_dim,)), ((), ())),
        precision=lax.Precision.HIGHEST,
        preferred_element_type=jnp.float32,
    )


def inverse_or_zero(scale):
    return jnp.where(scale > 0, 1.0 / jnp.where(scale > 0, scale, 1.0), 0.0)


def largest(value):
    return jnp.max(jnp.max(jnp.abs(value), axis=0, keepdims=True), axis=1, keepdims=True)


def split_kernel(h_ref, t_ref, out_ref):
    groups, _, half2, lanes = out_ref.shape
    half = half2 // 2
    for at, ref in ((0, h_ref), (half, t_ref)):
        for g in range(groups):
            for part in range(2):
                out_ref[g, part, at : at + half, :] = ref[
                    part * half : (part + 1) * half, g * lanes : (g + 1) * lanes
                ]


def block_of(ht_ref, part, which):
    groups, _, half2, lanes = ht_ref.shape
    half = half2 // 2
    block = ht_ref[:, part, which * half : (which + 1) * half, :]
    return block.reshape(groups * half, lanes)


def columns_kernel(core_ref, ht_ref, own_ref, other_ref, out_ref):
    first = core_ref[0] == 0
    own, other = own_ref[...], other_ref[...]
    out_ref[...] = dot(block_of(ht_ref, 0, 0), jnp.where(first, own, other)) + dot(
        block_of(ht_ref, 1, 0), jnp.where(first, other, own)
    )


def sum_kernel(in_ref, out_ref, *, rows):
    for at in range(0, rows, SUB):
        tiles = [in_ref[i + at : i + at + SUB, :] for i in range(0, in_ref.shape[0], rows)]
        while len(tiles) > 1:
            tiles = [a + b for a, b in zip(tiles[::2], tiles[1::2])]
        for i in range(0, out_ref.shape[0], rows):
            out_ref[i + at : i + at + SUB, :] = tiles[0]


def across_kernel(ht_ref, c_ref, out_ref):
    c = c_ref[...]
    scale = largest(c)
    c = c * inverse_or_zero(scale)
    for part in range(2):
        out_ref[part * LANE : (part + 1) * LANE, :] = dot(block_of(ht_ref, part, 0), c, 0, 0)
    out_ref[2 * LANE :, :] = jnp.broadcast_to(scale, (SUB, LANE))


def image_kernel(ht_ref, own_ref, other_ref, out_ref):
    scale, scale_other = own_ref[2 * LANE : 2 * LANE + 1, :], other_ref[2 * LANE : 2 * LANE + 1, :]
    top = inverse_or_zero(jnp.maximum(scale, scale_other))
    x = own_ref[: 2 * LANE, :] * (scale * top) + other_ref[: 2 * LANE, :] * (scale_other * top)
    rows = out_ref.shape[0] // 2
    for which in range(2):
        out_ref[which * rows : (which + 1) * rows, :] = dot(
            block_of(ht_ref, 0, which), x[:LANE]
        ) + dot(block_of(ht_ref, 1, which), x[LANE:])


def gram_kernel(at_ref, yz_ref, c_ref, own_ref, other_ref, out_ref, *, half):
    scale, scale_other = own_ref[2 * LANE : 2 * LANE + 1, :], other_ref[2 * LANE : 2 * LANE + 1, :]
    top = inverse_or_zero(jnp.maximum(scale, scale_other))
    c = c_ref[...]
    c = c * (inverse_or_zero(scale) * (scale * top))
    rows = yz_ref.shape[0] // 2
    y = yz_ref[:rows, :]
    y_scale = largest(y)
    back = inverse_or_zero(y_scale)
    y = y * back
    out_ref[:LANE, :] = dot(y, y, 0, 0)
    out_ref[LANE : 2 * LANE, :] = dot(y, yz_ref[rows:, :], 0, 0)
    out_ref[2 * LANE : 3 * LANE, :] = dot(c, y, 0, 0)
    start = pl.multiple_of(at_ref[0] * half, half)
    out_ref[3 * LANE : 3 * LANE + half, :] = yz_ref[pl.ds(start, half), :] * back
    out_ref[3 * LANE + half :, :] = jnp.broadcast_to(y_scale, (SUB, LANE))


def inverse_factors(matrices):
    size = matrices[0].shape[0]
    blocks = size // SUB
    lane = lax.broadcasted_iota(jnp.int32, (SUB, size), 1)
    sub = lax.broadcasted_iota(jnp.int32, (SUB, size), 0)
    work = [[m[SUB * i : SUB * (i + 1), :] for i in range(blocks)] for m in matrices]

    def columns(rows, low):
        return [
            jnp.broadcast_to(rows[:, low + j : low + j + 1], (SUB, size)) for j in range(SUB)
        ]

    def row(values, j):
        return jnp.broadcast_to(values[j : j + 1, :], (SUB, size))

    for k in range(blocks):
        low = SUB * k
        inside = (lane >= low) & (lane < low + SUB)
        done = []
        for mine in work:
            column = columns(mine[k], low)
            w = jnp.where(inside, (lane == sub + low).astype(jnp.float32), mine[k])
            steps, pivots = [], jnp.ones((SUB, size), jnp.float32)
            for j in range(SUB):
                pivot = row(column[j], j)
                inverse = 1.0 / pivot
                pivots = jnp.where(sub == j, pivot, pivots)
                factor = jnp.where(sub > j, column[j] * inverse, 0.0)
                ahead = {}
                for i in range(j + 1, SUB):
                    ahead[i] = row(column[i], j)
                    column[i] = column[i] - factor * ahead[i]
                reduced = row(w, j)
                w = w - factor * reduced
                steps.append((inverse, ahead, reduced))
            root = lax.rsqrt(pivots)
            root = root * (1.5 - 0.5 * pivots * root * root)
            mine[k] = jnp.where(lane <= sub + low, w * root, 0.0)
            done.append(steps)
        for mine, steps in zip(work, done):
            for i in range(k + 1, blocks):
                column = columns(mine[i], low)
                w = jnp.where(inside, 0.0, mine[i])
                for j, (inverse, ahead, reduced) in enumerate(steps):
                    factor = column[j] * inverse
                    for n in range(j + 1, SUB):
                        column[n] = column[n] - factor * ahead[n]
                    w = w - factor * reduced
                mine[i] = w
    return [jnp.concatenate(mine, axis=0) for mine in work]


def final_kernel(core_ref, own_ref, other_ref, basis_ref, operator_ref, *, half, total):
    at = 3 * LANE + half
    scale, scale_other = own_ref[at : at + 1, :], other_ref[at : at + 1, :]
    top = jnp.maximum(scale, scale_other)
    back = inverse_or_zero(top)
    f, f_other = scale * back, scale_other * back
    gram = own_ref[:LANE, :] * (f * f) + other_ref[:LANE, :] * (f_other * f_other)
    cross = own_ref[LANE : 2 * LANE, :] * f + other_ref[LANE : 2 * LANE, :] * f_other
    gram_w = own_ref[2 * LANE : 3 * LANE, :] * f + other_ref[2 * LANE : 3 * LANE, :] * f_other
    lower, lower_w = inverse_factors([gram, gram_w])
    root = jnp.sqrt(jnp.float32(total))
    core = core_ref[0]
    for ref, factor, place in ((own_ref, f, core), (other_ref, f_other, 1 - core)):
        rows = ref[3 * LANE : at, :] * (factor * root)
        basis_ref[pl.ds(pl.multiple_of(place * half, half), half), :] = dot(rows, lower, 1, 1)
    operator_ref[...] = dot(dot(lower, cross), lower_w, 1, 1) * lax.rsqrt(top)


def exchanged_rows(values, axis):
    count = lax.axis_size(axis)
    return exchanged(values.reshape(count, -1, LANE), axis).reshape(values.shape)


def summed_over_chips(part, name):
    rows = part.shape[0] // lax.axis_size(PLANE)
    kernel = functools.partial(sum_kernel, rows=rows)
    line = (lax.axis_size("z") * rows, LANE)
    (copies,) = call(kernel, name + "_plane", [line], [], [exchanged_rows(part, PLANE)])
    (copies,) = call(kernel, name + "_line", [part.shape], [], [exchanged_rows(copies, "z")])
    return exchanged_rows(copies, PLANE)


def on_device(hankel, shifted, start_basis):
    rows_dev = hankel.shape[0]
    groups, half = lax.axis_size(ROWS), rows_dev // 2
    rows = groups * half
    core = lax.axis_index("core").astype(jnp.int32).reshape(1)
    place = lax.axis_index(ROWS).astype(jnp.int32).reshape(1)
    other_start = from_other_core(start_basis)
    (pieces,) = call(split_kernel, "split", [(groups, 2, rows_dev, LANE)], [], [hankel, shifted])
    pieces = exchanged(pieces.reshape(2 * groups, rows_dev, LANE), CHANGE)
    ht = pieces.reshape(groups, 2, rows_dev, LANE)
    (c_part,) = call(
        columns_kernel, "columns", [(rows, LANE)], [core], [ht, start_basis, other_start]
    )
    c = summed_over_chips(c_part, "columns")
    (x_part,) = call(across_kernel, "across", [(2 * LANE + SUB, LANE)], [], [ht, c])
    x_other = from_other_core(x_part)
    (yz_part,) = call(image_kernel, "image", [(2 * rows, LANE)], [], [ht, x_part, x_other])
    yz = summed_over_chips(yz_part, "image")
    (grams,) = call(
        functools.partial(gram_kernel, half=half),
        "grams",
        [(3 * LANE + half + SUB, LANE)],
        [place],
        [yz, c, x_part, x_other],
    )
    return call(
        functools.partial(final_kernel, half=half, total=rows_dev * groups),
        "factors",
        [(rows_dev, LANE), (LANE, LANE)],
        [core],
        [grams, from_other_core(grams)],
    )


def solution(mesh):
    finer = Mesh(mesh.devices.reshape(4, 8, 4, 2), ("x", "z", "y", "core"))
    placed = (P(ROWS, COLS), P(ROWS, COLS), P((*COLS, *ROWS), None))

    def whole(*blocks):
        return tuple(on_device(*blocks))

    return jax.shard_map(
        whole, mesh=finer, in_specs=placed, out_specs=(P(ROWS, None), P()), check_vma=False
    )
```

```python
import functools

import jax
import jax.numpy as jnp
from jax import lax
from jax.experimental import pallas as pl
from jax.experimental.pallas import tpu as pltpu
from jax.sharding import Mesh
from jax.sharding import PartitionSpec as P

ROWS = ("x", "z")
COLS = ("y", "core")
PLANE = ("x", "y")
CHANGE = ("x", "z", "core")
SUB, LANE = 8, 128
PIECES = 4


def exchanged(blocks, axis):
    return lax.all_to_all(blocks, axis, 0, 0, tiled=True)


def from_other_core(value):
    return lax.ppermute(value, "core", [(0, 1), (1, 0)])


def call(kernel, name, shapes, arrays, scratch=(), space=pltpu.VMEM):
    return pl.pallas_call(
        kernel,
        name=name,
        out_shape=[jax.ShapeDtypeStruct(shape, jnp.float32) for shape in shapes],
        in_specs=[pl.BlockSpec(memory_space=space)] * len(arrays),
        out_specs=[pl.BlockSpec(memory_space=space)] * len(shapes),
        scratch_shapes=scratch,
        compiler_params=pltpu.CompilerParams(vmem_limit_bytes=(24 if space is pltpu.VMEM else 60) << 20),
    )(*arrays)


def dot(left, right, left_dim=1, right_dim=0):
    return lax.dot_general(
        left,
        right,
        (((left_dim,), (right_dim,)), ((), ())),
        precision=lax.Precision.HIGHEST,
        preferred_element_type=jnp.float32,
    )


def inverse_or_zero(scale):
    return jnp.where(scale > 0, 1.0 / jnp.where(scale > 0, scale, 1.0), 0.0)


def largest(value):
    return jnp.max(jnp.max(jnp.abs(value), axis=0, keepdims=True), axis=1, keepdims=True)


def split_kernel(h_ref, t_ref, out_ref, h, t, out, in_sem, out_sem):
    groups, _, half2, lanes = out.shape
    half, some = half2 // 2, groups // PIECES
    loads, stores = [], []
    for i in range(PIECES):
        at = slice(i * some * lanes, (i + 1) * some * lanes)
        for j, (source, block) in enumerate(((h_ref, h), (t_ref, t))):
            load = pltpu.make_async_copy(source.at[:, at], block.at[:, at], in_sem.at[2 * i + j])
            load.start()
            loads.append(load)
    for i in range(PIECES):
        for j, block in enumerate((h, t)):
            loads[2 * i + j].wait()
            for g in range(i * some, (i + 1) * some):
                for part in range(2):
                    out[g, part, j * half : (j + 1) * half, :] = block[
                        part * half : (part + 1) * half, g * lanes : (g + 1) * lanes
                    ]
        at = slice(i * some, (i + 1) * some)
        store = pltpu.make_async_copy(out.at[at], out_ref.at[at], out_sem.at[i])
        store.start()
        stores.append(store)
    for store in stores:
        store.wait()


def block_of(ht_ref, part, which):
    groups, _, half2, lanes = ht_ref.shape
    half = half2 // 2
    block = ht_ref[:, part, which * half : (which + 1) * half, :]
    return block.reshape(groups * half, lanes)


def columns_kernel(ht_ref, own_ref, other_ref, out_ref):
    first = lax.axis_index("core") == 0
    own, other = own_ref[...], other_ref[...]
    out_ref[...] = dot(block_of(ht_ref, 0, 0), jnp.where(first, own, other)) + dot(
        block_of(ht_ref, 1, 0), jnp.where(first, other, own)
    )


def sum_kernel(in_ref, out_ref, *, rows):
    for at in range(0, rows, SUB):
        tiles = [in_ref[i + at : i + at + SUB, :] for i in range(0, in_ref.shape[0], rows)]
        while len(tiles) > 1:
            tiles = [a + b for a, b in zip(tiles[::2], tiles[1::2])]
        for i in range(0, out_ref.shape[0], rows):
            out_ref[i + at : i + at + SUB, :] = tiles[0]


def across_kernel(ht_ref, c_ref, out_ref):
    c = c_ref[...]
    scale = largest(c)
    c = c * inverse_or_zero(scale)
    for part in range(2):
        out_ref[part * LANE : (part + 1) * LANE, :] = dot(block_of(ht_ref, part, 0), c, 0, 0)
    out_ref[2 * LANE :, :] = jnp.broadcast_to(scale, (SUB, LANE))


def image_kernel(ht_ref, own_ref, other_ref, out_ref):
    scale, scale_other = own_ref[2 * LANE : 2 * LANE + 1, :], other_ref[2 * LANE : 2 * LANE + 1, :]
    top = inverse_or_zero(jnp.maximum(scale, scale_other))
    x = own_ref[: 2 * LANE, :] * (scale * top) + other_ref[: 2 * LANE, :] * (scale_other * top)
    rows = out_ref.shape[0] // 2
    for which in range(2):
        out_ref[which * rows : (which + 1) * rows, :] = dot(
            block_of(ht_ref, 0, which), x[:LANE]
        ) + dot(block_of(ht_ref, 1, which), x[LANE:])


def gram_kernel(yz_ref, c_ref, own_ref, other_ref, out_ref, *, half):
    scale, scale_other = own_ref[2 * LANE : 2 * LANE + 1, :], other_ref[2 * LANE : 2 * LANE + 1, :]
    top = inverse_or_zero(jnp.maximum(scale, scale_other))
    c = c_ref[...]
    c = c * (inverse_or_zero(scale) * (scale * top))
    rows = yz_ref.shape[0] // 2
    y = yz_ref[:rows, :]
    y_scale = largest(y)
    back = inverse_or_zero(y_scale)
    y = y * back
    out_ref[:LANE, :] = dot(y, y, 0, 0)
    out_ref[LANE : 2 * LANE, :] = dot(y, yz_ref[rows:, :], 0, 0)
    out_ref[2 * LANE : 3 * LANE, :] = dot(c, y, 0, 0)
    place = lax.axis_index("x") * lax.axis_size("z") + lax.axis_index("z")
    start = pl.multiple_of(place * half, half)
    out_ref[3 * LANE : 3 * LANE + half, :] = yz_ref[pl.ds(start, half), :] * back
    out_ref[3 * LANE + half :, :] = jnp.broadcast_to(y_scale, (SUB, LANE))


def inverse_factors(matrices):
    size = matrices[0].shape[0]
    blocks = size // SUB
    lane = lax.broadcasted_iota(jnp.int32, (SUB, size), 1)
    sub = lax.broadcasted_iota(jnp.int32, (SUB, size), 0)
    work = [[m[SUB * i : SUB * (i + 1), :] for i in range(blocks)] for m in matrices]

    def columns(rows, low):
        return [
            jnp.broadcast_to(rows[:, low + j : low + j + 1], (SUB, size)) for j in range(SUB)
        ]

    def row(values, j):
        return jnp.broadcast_to(values[j : j + 1, :], (SUB, size))

    for k in range(blocks):
        low = SUB * k
        inside = (lane >= low) & (lane < low + SUB)
        done = []
        for mine in work:
            column = columns(mine[k], low)
            w = jnp.where(inside, (lane == sub + low).astype(jnp.float32), mine[k])
            steps, pivots = [], jnp.ones((SUB, size), jnp.float32)
            for j in range(SUB):
                pivot = row(column[j], j)
                inverse = 1.0 / pivot
                pivots = jnp.where(sub == j, pivot, pivots)
                factor = jnp.where(sub > j, column[j] * inverse, 0.0)
                ahead = {}
                for i in range(j + 1, SUB):
                    ahead[i] = row(column[i], j)
                    column[i] = column[i] - factor * ahead[i]
                reduced = row(w, j)
                w = w - factor * reduced
                steps.append((inverse, ahead, reduced))
            root = lax.rsqrt(pivots)
            root = root * (1.5 - 0.5 * pivots * root * root)
            mine[k] = jnp.where(lane <= sub + low, w * root, 0.0)
            done.append(steps)
        for mine, steps in zip(work, done):
            for i in range(k + 1, blocks):
                column = columns(mine[i], low)
                w = jnp.where(inside, 0.0, mine[i])
                for j, (inverse, ahead, reduced) in enumerate(steps):
                    factor = column[j] * inverse
                    for n in range(j + 1, SUB):
                        column[n] = column[n] - factor * ahead[n]
                    w = w - factor * reduced
                mine[i] = w
    return [jnp.concatenate(mine, axis=0) for mine in work]


def final_kernel(own_ref, other_ref, basis_ref, operator_ref, *, half, total):
    at = 3 * LANE + half
    scale, scale_other = own_ref[at : at + 1, :], other_ref[at : at + 1, :]
    top = jnp.maximum(scale, scale_other)
    back = inverse_or_zero(top)
    f, f_other = scale * back, scale_other * back
    gram = own_ref[:LANE, :] * (f * f) + other_ref[:LANE, :] * (f_other * f_other)
    cross = own_ref[LANE : 2 * LANE, :] * f + other_ref[LANE : 2 * LANE, :] * f_other
    gram_w = own_ref[2 * LANE : 3 * LANE, :] * f + other_ref[2 * LANE : 3 * LANE, :] * f_other
    lower, lower_w = inverse_factors([gram, gram_w])
    root = jnp.sqrt(jnp.float32(total))
    core = lax.axis_index("core")
    for ref, factor, place in ((own_ref, f, core), (other_ref, f_other, 1 - core)):
        rows = ref[3 * LANE : at, :] * (factor * root)
        basis_ref[pl.ds(pl.multiple_of(place * half, half), half), :] = dot(rows, lower, 1, 1)
    operator_ref[...] = dot(dot(lower, cross), lower_w, 1, 1) * lax.rsqrt(top)


def exchanged_rows(values, axis):
    count = lax.axis_size(axis)
    return exchanged(values.reshape(count, -1, LANE), axis).reshape(values.shape)


def summed_over_chips(part, name):
    rows = part.shape[0] // lax.axis_size(PLANE)
    kernel = functools.partial(sum_kernel, rows=rows)
    line = (lax.axis_size("z") * rows, LANE)
    (copies,) = call(kernel, name + "_plane", [line], [exchanged_rows(part, PLANE)])
    (copies,) = call(kernel, name + "_line", [part.shape], [exchanged_rows(copies, "z")])
    return exchanged_rows(copies, PLANE)


def on_device(hankel, shifted, start_basis):
    rows_dev = hankel.shape[0]
    groups, half = lax.axis_size(ROWS), rows_dev // 2
    rows = groups * half
    other_start = from_other_core(start_basis)
    out_shape = (groups, 2, rows_dev, LANE)
    scratch = [
        pltpu.VMEM(hankel.shape, jnp.float32),
        pltpu.VMEM(hankel.shape, jnp.float32),
        pltpu.VMEM(out_shape, jnp.float32),
        pltpu.SemaphoreType.DMA((2 * PIECES,)),
        pltpu.SemaphoreType.DMA((PIECES,)),
    ]
    (pieces,) = call(split_kernel, "split", [out_shape], [hankel, shifted], scratch, pl.ANY)
    pieces = exchanged(pieces.reshape(2 * groups, rows_dev, LANE), CHANGE)
    ht = pieces.reshape(groups, 2, rows_dev, LANE)
    (c_part,) = call(columns_kernel, "columns", [(rows, LANE)], [ht, start_basis, other_start])
    c = summed_over_chips(c_part, "columns")
    (x_part,) = call(across_kernel, "across", [(2 * LANE + SUB, LANE)], [ht, c])
    x_other = from_other_core(x_part)
    (yz_part,) = call(image_kernel, "image", [(2 * rows, LANE)], [ht, x_part, x_other])
    yz = summed_over_chips(yz_part, "image")
    (grams,) = call(
        functools.partial(gram_kernel, half=half),
        "grams",
        [(3 * LANE + half + SUB, LANE)],
        [yz, c, x_part, x_other],
    )
    return call(
        functools.partial(final_kernel, half=half, total=rows_dev * groups),
        "factors",
        [(rows_dev, LANE), (LANE, LANE)],
        [grams, from_other_core(grams)],
    )


def solution(mesh):
    finer = Mesh(mesh.devices.reshape(4, 8, 4, 2), ("x", "z", "y", "core"))
    placed = (P(ROWS, COLS), P(ROWS, COLS), P((*COLS, *ROWS), None))

    def whole(*blocks):
        return tuple(on_device(*blocks))

    return jax.shard_map(
        whole, mesh=finer, in_specs=placed, out_specs=(P(ROWS, None), P()), check_vma=False
    )
```

```python
import functools

import jax
import jax.numpy as jnp
from jax import lax
from jax.experimental import pallas as pl
from jax.experimental.pallas import tpu as pltpu
from jax.sharding import Mesh
from jax.sharding import PartitionSpec as P

ROWS = ("x", "z")
COLS = ("y", "core")
PLANE = ("x", "y")
CHANGE = ("x", "z", "core")
SUB, LANE = 8, 128
PIECES = 4


def exchanged(blocks, axis):
    return lax.all_to_all(blocks, axis, 0, 0, tiled=True)


def from_other_core(value):
    return lax.ppermute(value, "core", [(0, 1), (1, 0)])


def call(kernel, name, shapes, arrays, scratch=(), space=pltpu.VMEM):
    return pl.pallas_call(
        kernel,
        name=name,
        out_shape=[jax.ShapeDtypeStruct(shape, jnp.float32) for shape in shapes],
        in_specs=[pl.BlockSpec(memory_space=space)] * len(arrays),
        out_specs=[pl.BlockSpec(memory_space=pltpu.VMEM)] * len(shapes),
        scratch_shapes=scratch,
        compiler_params=pltpu.CompilerParams(vmem_limit_bytes=(24 if space is pltpu.VMEM else 60) << 20),
    )(*arrays)


def dot(left, right, left_dim=1, right_dim=0):
    return lax.dot_general(
        left,
        right,
        (((left_dim,), (right_dim,)), ((), ())),
        precision=lax.Precision.HIGHEST,
        preferred_element_type=jnp.float32,
    )


def inverse_or_zero(scale):
    return jnp.where(scale > 0, 1.0 / jnp.where(scale > 0, scale, 1.0), 0.0)


def largest(value):
    return jnp.max(jnp.max(jnp.abs(value), axis=0, keepdims=True), axis=1, keepdims=True)


def split_kernel(h_ref, t_ref, out_ref, h, t, sem):
    groups, _, half2, lanes = out_ref.shape
    half, some = half2 // 2, groups // PIECES
    loads = []
    for i in range(PIECES):
        at = slice(i * some * lanes, (i + 1) * some * lanes)
        for j, (source, block) in enumerate(((h_ref, h), (t_ref, t))):
            load = pltpu.make_async_copy(source.at[:, at], block.at[:, at], sem.at[2 * i + j])
            load.start()
            loads.append(load)
    for i in range(PIECES):
        for j, block in enumerate((h, t)):
            loads[2 * i + j].wait()
            for g in range(i * some, (i + 1) * some):
                for part in range(2):
                    out_ref[g, part, j * half : (j + 1) * half, :] = block[
                        part * half : (part + 1) * half, g * lanes : (g + 1) * lanes
                    ]


def block_of(ht_ref, part, which):
    groups, _, half2, lanes = ht_ref.shape
    half = half2 // 2
    block = ht_ref[:, part, which * half : (which + 1) * half, :]
    return block.reshape(groups * half, lanes)


def columns_kernel(ht_ref, own_ref, other_ref, out_ref):
    first = lax.axis_index("core") == 0
    own, other = own_ref[...], other_ref[...]
    out_ref[...] = dot(block_of(ht_ref, 0, 0), jnp.where(first, own, other)) + dot(
        block_of(ht_ref, 1, 0), jnp.where(first, other, own)
    )


def sum_kernel(in_ref, out_ref, *, rows):
    for at in range(0, rows, SUB):
        tiles = [in_ref[i + at : i + at + SUB, :] for i in range(0, in_ref.shape[0], rows)]
        while len(tiles) > 1:
            tiles = [a + b for a, b in zip(tiles[::2], tiles[1::2])]
        for i in range(0, out_ref.shape[0], rows):
            out_ref[i + at : i + at + SUB, :] = tiles[0]


def across_kernel(ht_ref, c_ref, out_ref):
    c = c_ref[...]
    scale = largest(c)
    c = c * inverse_or_zero(scale)
    for part in range(2):
        out_ref[part * LANE : (part + 1) * LANE, :] = dot(block_of(ht_ref, part, 0), c, 0, 0)
    out_ref[2 * LANE :, :] = jnp.broadcast_to(scale, (SUB, LANE))


def image_kernel(ht_ref, own_ref, other_ref, out_ref):
    scale, scale_other = own_ref[2 * LANE : 2 * LANE + 1, :], other_ref[2 * LANE : 2 * LANE + 1, :]
    top = inverse_or_zero(jnp.maximum(scale, scale_other))
    x = own_ref[: 2 * LANE, :] * (scale * top) + other_ref[: 2 * LANE, :] * (scale_other * top)
    rows = out_ref.shape[0] // 2
    for which in range(2):
        out_ref[which * rows : (which + 1) * rows, :] = dot(
            block_of(ht_ref, 0, which), x[:LANE]
        ) + dot(block_of(ht_ref, 1, which), x[LANE:])


def gram_kernel(yz_ref, c_ref, own_ref, other_ref, out_ref, *, half):
    scale, scale_other = own_ref[2 * LANE : 2 * LANE + 1, :], other_ref[2 * LANE : 2 * LANE + 1, :]
    top = inverse_or_zero(jnp.maximum(scale, scale_other))
    c = c_ref[...]
    c = c * (inverse_or_zero(scale) * (scale * top))
    rows = yz_ref.shape[0] // 2
    y = yz_ref[:rows, :]
    y_scale = largest(y)
    back = inverse_or_zero(y_scale)
    y = y * back
    out_ref[:LANE, :] = dot(y, y, 0, 0)
    out_ref[LANE : 2 * LANE, :] = dot(y, yz_ref[rows:, :], 0, 0)
    out_ref[2 * LANE : 3 * LANE, :] = dot(c, y, 0, 0)
    place = lax.axis_index("x") * lax.axis_size("z") + lax.axis_index("z")
    start = pl.multiple_of(place * half, half)
    out_ref[3 * LANE : 3 * LANE + half, :] = yz_ref[pl.ds(start, half), :] * back
    out_ref[3 * LANE + half :, :] = jnp.broadcast_to(y_scale, (SUB, LANE))


def inverse_factors(matrices):
    size = matrices[0].shape[0]
    blocks = size // SUB
    lane = lax.broadcasted_iota(jnp.int32, (SUB, size), 1)
    sub = lax.broadcasted_iota(jnp.int32, (SUB, size), 0)
    work = [[m[SUB * i : SUB * (i + 1), :] for i in range(blocks)] for m in matrices]

    def columns(rows, low):
        return [
            jnp.broadcast_to(rows[:, low + j : low + j + 1], (SUB, size)) for j in range(SUB)
        ]

    def row(values, j):
        return jnp.broadcast_to(values[j : j + 1, :], (SUB, size))

    for k in range(blocks):
        low = SUB * k
        inside = (lane >= low) & (lane < low + SUB)
        done = []
        for mine in work:
            column = columns(mine[k], low)
            w = jnp.where(inside, (lane == sub + low).astype(jnp.float32), mine[k])
            steps, pivots = [], jnp.ones((SUB, size), jnp.float32)
            for j in range(SUB):
                pivot = row(column[j], j)
                inverse = 1.0 / pivot
                pivots = jnp.where(sub == j, pivot, pivots)
                factor = jnp.where(sub > j, column[j] * inverse, 0.0)
                ahead = {}
                for i in range(j + 1, SUB):
                    ahead[i] = row(column[i], j)
                    column[i] = column[i] - factor * ahead[i]
                reduced = row(w, j)
                w = w - factor * reduced
                steps.append((inverse, ahead, reduced))
            root = lax.rsqrt(pivots)
            root = root * (1.5 - 0.5 * pivots * root * root)
            mine[k] = jnp.where(lane <= sub + low, w * root, 0.0)
            done.append(steps)
        for mine, steps in zip(work, done):
            for i in range(k + 1, blocks):
                column = columns(mine[i], low)
                w = jnp.where(inside, 0.0, mine[i])
                for j, (inverse, ahead, reduced) in enumerate(steps):
                    factor = column[j] * inverse
                    for n in range(j + 1, SUB):
                        column[n] = column[n] - factor * ahead[n]
                    w = w - factor * reduced
                mine[i] = w
    return [jnp.concatenate(mine, axis=0) for mine in work]


def final_kernel(own_ref, other_ref, basis_ref, operator_ref, *, half, total):
    at = 3 * LANE + half
    scale, scale_other = own_ref[at : at + 1, :], other_ref[at : at + 1, :]
    top = jnp.maximum(scale, scale_other)
    back = inverse_or_zero(top)
    f, f_other = scale * back, scale_other * back
    gram = own_ref[:LANE, :] * (f * f) + other_ref[:LANE, :] * (f_other * f_other)
    cross = own_ref[LANE : 2 * LANE, :] * f + other_ref[LANE : 2 * LANE, :] * f_other
    gram_w = own_ref[2 * LANE : 3 * LANE, :] * f + other_ref[2 * LANE : 3 * LANE, :] * f_other
    lower, lower_w = inverse_factors([gram, gram_w])
    root = jnp.sqrt(jnp.float32(total))
    rows = jnp.concatenate(
        [own_ref[3 * LANE : at, :] * (f * root), other_ref[3 * LANE : at, :] * (f_other * root)]
    )
    basis = dot(rows, lower, 1, 1)
    core = lax.axis_index("core")
    for block, place in ((basis[:half], core), (basis[half:], 1 - core)):
        basis_ref[pl.ds(pl.multiple_of(place * half, half), half), :] = block
    operator_ref[...] = dot(dot(lower, cross), lower_w, 1, 1) * lax.rsqrt(top)


def exchanged_rows(values, axis):
    count = lax.axis_size(axis)
    return exchanged(values.reshape(count, -1, LANE), axis).reshape(values.shape)


def summed_over_chips(part, name):
    rows = part.shape[0] // lax.axis_size(PLANE)
    kernel = functools.partial(sum_kernel, rows=rows)
    line = (lax.axis_size("z") * rows, LANE)
    (copies,) = call(kernel, name + "_plane", [line], [exchanged_rows(part, PLANE)])
    (copies,) = call(kernel, name + "_line", [part.shape], [exchanged_rows(copies, "z")])
    return exchanged_rows(copies, PLANE)


def on_device(hankel, shifted, start_basis):
    rows_dev = hankel.shape[0]
    groups, half = lax.axis_size(ROWS), rows_dev // 2
    rows = groups * half
    other_start = from_other_core(start_basis)
    out_shape = (groups, 2, rows_dev, LANE)
    scratch = [
        pltpu.VMEM(hankel.shape, jnp.float32),
        pltpu.VMEM(hankel.shape, jnp.float32),
        pltpu.SemaphoreType.DMA((2 * PIECES,)),
    ]
    (pieces,) = call(split_kernel, "split", [out_shape], [hankel, shifted], scratch, pl.ANY)
    pieces, other_start = lax.optimization_barrier((pieces, other_start))
    pieces = exchanged(pieces.reshape(2 * groups, rows_dev, LANE), CHANGE)
    ht = pieces.reshape(groups, 2, rows_dev, LANE)
    (c_part,) = call(columns_kernel, "columns", [(rows, LANE)], [ht, start_basis, other_start])
    c = summed_over_chips(c_part, "columns")
    (x_part,) = call(across_kernel, "across", [(2 * LANE + SUB, LANE)], [ht, c])
    x_other = from_other_core(x_part)
    (yz_part,) = call(image_kernel, "image", [(2 * rows, LANE)], [ht, x_part, x_other])
    yz = summed_over_chips(yz_part, "image")
    (grams,) = call(
        functools.partial(gram_kernel, half=half),
        "grams",
        [(3 * LANE + half + SUB, LANE)],
        [yz, c, x_part, x_other],
    )
    return call(
        functools.partial(final_kernel, half=half, total=rows_dev * groups),
        "factors",
        [(rows_dev, LANE), (LANE, LANE)],
        [grams, from_other_core(grams)],
    )


def solution(mesh):
    finer = Mesh(mesh.devices.reshape(4, 8, 4, 2), ("x", "z", "y", "core"))
    placed = (P(ROWS, COLS), P(ROWS, COLS), P((*COLS, *ROWS), None))

    def whole(*blocks):
        return tuple(on_device(*blocks))

    return jax.shard_map(
        whole, mesh=finer, in_specs=placed, out_specs=(P(ROWS, None), P()), check_vma=False
    )
```

```python
import functools

import jax
import jax.numpy as jnp
from jax import lax
from jax.experimental import pallas as pl
from jax.experimental.pallas import tpu as pltpu
from jax.sharding import Mesh
from jax.sharding import PartitionSpec as P

ROWS = ("x", "z")
COLS = ("y", "core")
PLANE = ("x", "y")
SUB, LANE = 8, 128
PIECES = 4


def exchanged(blocks, axis):
    return lax.all_to_all(blocks, axis, 0, 0, tiled=True)


def from_other_core(value):
    return lax.ppermute(value, "core", [(0, 1), (1, 0)])


def to_second(value):
    return lax.ppermute(value, "core", [(0, 1)])


def call(kernel, name, shapes, arrays, scratch=(), space=pltpu.VMEM):
    return pl.pallas_call(
        kernel,
        name=name,
        out_shape=[jax.ShapeDtypeStruct(shape, jnp.float32) for shape in shapes],
        in_specs=[pl.BlockSpec(memory_space=space)] * len(arrays),
        out_specs=[pl.BlockSpec(memory_space=space)] * len(shapes),
        scratch_shapes=scratch,
        compiler_params=pltpu.CompilerParams(vmem_limit_bytes=(24 if space is pltpu.VMEM else 60) << 20),
    )(*arrays)


def dot(left, right, left_dim=1, right_dim=0):
    return lax.dot_general(
        left,
        right,
        (((left_dim,), (right_dim,)), ((), ())),
        precision=lax.Precision.HIGHEST,
        preferred_element_type=jnp.float32,
    )


def inverse_or_zero(scale):
    return jnp.where(scale > 0, 1.0 / jnp.where(scale > 0, scale, 1.0), 0.0)


def largest(value):
    return jnp.max(jnp.max(jnp.abs(value), axis=0, keepdims=True), axis=1, keepdims=True)


def split_kernel(*refs):
    count = (len(refs) - 4) // 2
    sources, out_ref = refs[:count], refs[count]
    blocks, out, in_sem, out_sem = refs[count + 1 : 2 * count + 1], *refs[2 * count + 1 :]
    groups, _, lanes = out.shape
    some, rows = groups // PIECES, out.shape[1] // count
    loads, stores = [], []
    for i in range(PIECES):
        at = slice(i * some * lanes, (i + 1) * some * lanes)
        for j in range(count):
            load = pltpu.make_async_copy(
                sources[j].at[:, at], blocks[j].at[:, at], in_sem.at[count * i + j]
            )
            load.start()
            loads.append(load)
    for i in range(PIECES):
        for j in range(count):
            loads[count * i + j].wait()
            for g in range(i * some, (i + 1) * some):
                out[g, j * rows : (j + 1) * rows, :] = blocks[j][:, g * lanes : (g + 1) * lanes]
        at = slice(i * some, (i + 1) * some)
        store = pltpu.make_async_copy(out.at[at], out_ref.at[at], out_sem.at[i])
        store.start()
        stores.append(store)
    for store in stores:
        store.wait()


def columns_kernel(own_ref, other_ref, start_ref, start_other_ref, out_ref):
    out_ref[...] = dot(own_ref[...], start_ref[...]) + dot(other_ref[...], start_other_ref[...])


def sum_kernel(in_ref, out_ref, *, rows):
    for at in range(0, rows, SUB):
        tiles = [in_ref[i + at : i + at + SUB, :] for i in range(0, in_ref.shape[0], rows)]
        while len(tiles) > 1:
            tiles = [a + b for a, b in zip(tiles[::2], tiles[1::2])]
        for i in range(0, out_ref.shape[0], rows):
            out_ref[i + at : i + at + SUB, :] = tiles[0]


def across_kernel(own_ref, other_ref, c_ref, x_ref, out_ref, unused_ref):
    c = c_ref[...]
    c = c * inverse_or_zero(largest(c))
    x_ref[:LANE, :] = dot(own_ref[...], c, 0, 0)
    x_ref[LANE:, :] = dot(other_ref[...], c, 0, 0)
    out_ref[...] = c


def image_kernel(own_ref, other_ref, t_ref, x_ref, x_other_ref, out_ref):
    core = lax.axis_index("core")

    @pl.when(core == 0)
    def _():
        x = x_ref[...]
        out_ref[...] = dot(own_ref[...], x[:LANE]) + dot(other_ref[...], x[LANE:])

    @pl.when(core == 1)
    def _():
        x = x_other_ref[...]
        rows = t_ref.shape[1] // 2
        first = t_ref[:, :rows, :].reshape(out_ref.shape)
        second = t_ref[:, rows:, :].reshape(out_ref.shape)
        out_ref[...] = dot(first, x[:LANE]) + dot(second, x[LANE:])


def inverse_factors(matrices):
    size = matrices[0].shape[0]
    blocks = size // SUB
    lane = lax.broadcasted_iota(jnp.int32, (SUB, size), 1)
    sub = lax.broadcasted_iota(jnp.int32, (SUB, size), 0)
    work = [[m[SUB * i : SUB * (i + 1), :] for i in range(blocks)] for m in matrices]

    def columns(rows, low):
        return [
            jnp.broadcast_to(rows[:, low + j : low + j + 1], (SUB, size)) for j in range(SUB)
        ]

    def row(values, j):
        return jnp.broadcast_to(values[j : j + 1, :], (SUB, size))

    for k in range(blocks):
        low = SUB * k
        inside = (lane >= low) & (lane < low + SUB)
        done = []
        for mine in work:
            column = columns(mine[k], low)
            w = jnp.where(inside, (lane == sub + low).astype(jnp.float32), mine[k])
            steps, pivots = [], jnp.ones((SUB, size), jnp.float32)
            for j in range(SUB):
                pivot = row(column[j], j)
                inverse = 1.0 / pivot
                pivots = jnp.where(sub == j, pivot, pivots)
                factor = jnp.where(sub > j, column[j] * inverse, 0.0)
                ahead = {}
                for i in range(j + 1, SUB):
                    ahead[i] = row(column[i], j)
                    column[i] = column[i] - factor * ahead[i]
                reduced = row(w, j)
                w = w - factor * reduced
                steps.append((inverse, ahead, reduced))
            root = lax.rsqrt(pivots)
            root = root * (1.5 - 0.5 * pivots * root * root)
            mine[k] = jnp.where(lane <= sub + low, w * root, 0.0)
            done.append(steps)
        for mine, steps in zip(work, done):
            for i in range(k + 1, blocks):
                column = columns(mine[i], low)
                w = jnp.where(inside, 0.0, mine[i])
                for j, (inverse, ahead, reduced) in enumerate(steps):
                    factor = column[j] * inverse
                    for n in range(j + 1, SUB):
                        column[n] = column[n] - factor * ahead[n]
                    w = w - factor * reduced
                mine[i] = w
    return [jnp.concatenate(mine, axis=0) for mine in work]


def final_kernel(own_ref, other_ref, c_ref, c_other_ref, basis_ref, operator_ref, y_ref):
    first = lax.axis_index("core") == 0
    y = jnp.where(first, own_ref[...], other_ref[...])
    z = jnp.where(first, other_ref[...], own_ref[...])
    c = jnp.where(first, c_ref[...], c_other_ref[...])
    scale = largest(y)
    y = y * inverse_or_zero(scale)
    y_ref[...] = y
    lower, lower_w = inverse_factors([dot(y, y, 0, 0), dot(c, y, 0, 0)])
    cross = dot(y, z, 0, 0)
    rows, total = basis_ref.shape[0], y_ref.shape[0]
    place = lax.axis_index("x") * lax.axis_size("z") + lax.axis_index("z")
    mine = y_ref[pl.ds(pl.multiple_of(place * rows, rows), rows), :]
    basis_ref[...] = dot(mine * jnp.sqrt(jnp.float32(total)), lower, 1, 1)
    operator_ref[...] = dot(dot(lower, cross), lower_w, 1, 1) * lax.rsqrt(scale)


def exchanged_rows(values, axis):
    count = lax.axis_size(axis)
    return exchanged(values.reshape(count, -1, LANE), axis).reshape(values.shape)


def summed_over_chips(part, name):
    rows = part.shape[0] // lax.axis_size(PLANE)
    kernel = functools.partial(sum_kernel, rows=rows)
    line = (lax.axis_size("z") * rows, LANE)
    (copies,) = call(kernel, name + "_plane", [line], [exchanged_rows(part, PLANE)])
    (copies,) = call(kernel, name + "_line", [part.shape], [exchanged_rows(copies, "z")])
    return exchanged_rows(copies, PLANE)


def split(name, *sources):
    rows, cols = sources[0].shape
    shape = (lax.axis_size(ROWS), len(sources) * rows, LANE)
    scratch = [pltpu.VMEM((rows, cols), jnp.float32)] * len(sources) + [
        pltpu.VMEM(shape, jnp.float32),
        pltpu.SemaphoreType.DMA((len(sources) * PIECES,)),
        pltpu.SemaphoreType.DMA((PIECES,)),
    ]
    return call(split_kernel, name, [shape], sources, scratch, pl.ANY)[0]


def on_device(hankel, shifted, start_basis):
    groups, rows_dev = lax.axis_size(ROWS), hankel.shape[0]
    rows = groups * rows_dev
    start_other = from_other_core(start_basis)
    shifted_other = to_second(shifted)
    own = exchanged(split("split", hankel), ROWS).reshape(rows, LANE)
    other = lax.ppermute(own, "core", [(1, 0)])
    both = (groups, 2 * rows_dev, LANE)

    def project(own, other, start_basis, start_other, shifted, shifted_other):
        (c_part,) = call(
            columns_kernel, "columns", [(rows, LANE)], [own, other, start_basis, start_other]
        )
        c = summed_over_chips(c_part, "columns")
        shapes = [(2 * LANE, LANE), (rows, LANE), both]
        return tuple(call(across_kernel, "across", shapes, [own, other, c]))

    def relay(own, other, start_basis, start_other, shifted, shifted_other):
        t = exchanged(split("split_shifted", shifted_other, shifted), ROWS)
        return jnp.zeros((2 * LANE, LANE), jnp.float32), jnp.zeros((rows, LANE), jnp.float32), t

    x, c, t = lax.cond(
        lax.axis_index("core") == 0, project, relay,
        own, other, start_basis, start_other, shifted, shifted_other,
    )
    x_other, c_other = to_second(x), to_second(c)
    (part,) = call(image_kernel, "image", [(rows, LANE)], [own, other, t, x, x_other])
    part = summed_over_chips(part, "image")
    return call(
        final_kernel,
        "factors",
        [(rows_dev, LANE), (LANE, LANE)],
        [part, from_other_core(part), c, c_other],
        [pltpu.VMEM((rows, LANE), jnp.float32)],
    )


def solution(mesh):
    finer = Mesh(mesh.devices.reshape(4, 8, 4, 2), ("x", "z", "y", "core"))
    placed = (P(ROWS, COLS), P(ROWS, COLS), P((*COLS, *ROWS), None))

    def whole(*blocks):
        return tuple(on_device(*blocks))

    return jax.shard_map(
        whole, mesh=finer, in_specs=placed, out_specs=(P(ROWS, None), P()), check_vma=False
    )
```

```python
import functools

import jax
import jax.numpy as jnp
from jax import lax
from jax.experimental import pallas as pl
from jax.experimental.pallas import tpu as pltpu
from jax.sharding import Mesh
from jax.sharding import PartitionSpec as P

ROWS = ("x", "z")
COLS = ("y", "core")
PLANE = ("x", "y")
SUB, LANE = 8, 128
PIECES = 4


def exchanged(blocks, axis):
    return lax.all_to_all(blocks, axis, 0, 0, tiled=True)


def from_other_core(value):
    return lax.ppermute(value, "core", [(0, 1), (1, 0)])


def to_second(value):
    return lax.ppermute(value, "core", [(0, 1)])


def call(kernel, name, shapes, arrays, scratch=(), space=pltpu.VMEM):
    return pl.pallas_call(
        kernel,
        name=name,
        out_shape=[jax.ShapeDtypeStruct(shape, jnp.float32) for shape in shapes],
        in_specs=[pl.BlockSpec(memory_space=space)] * len(arrays),
        out_specs=[pl.BlockSpec(memory_space=space)] * len(shapes),
        scratch_shapes=scratch,
        compiler_params=pltpu.CompilerParams(vmem_limit_bytes=(24 if space is pltpu.VMEM else 60) << 20),
    )(*arrays)


def dot(left, right, left_dim=1, right_dim=0):
    return lax.dot_general(
        left,
        right,
        (((left_dim,), (right_dim,)), ((), ())),
        precision=lax.Precision.HIGHEST,
        preferred_element_type=jnp.float32,
    )


def inverse_or_zero(scale):
    return jnp.where(scale > 0, 1.0 / jnp.where(scale > 0, scale, 1.0), 0.0)


def largest(value):
    return jnp.max(jnp.max(jnp.abs(value), axis=0, keepdims=True), axis=1, keepdims=True)


def split_kernel(*refs):
    count = (len(refs) - 4) // 2
    sources, out_ref = refs[:count], refs[count]
    blocks, out, in_sem, out_sem = refs[count + 1 : 2 * count + 1], *refs[2 * count + 1 :]
    groups, _, lanes = out.shape
    some, rows = groups // PIECES, out.shape[1] // count
    loads, stores = [], []
    for i in range(PIECES):
        at = slice(i * some * lanes, (i + 1) * some * lanes)
        for j in range(count):
            load = pltpu.make_async_copy(
                sources[j].at[:, at], blocks[j].at[:, at], in_sem.at[count * i + j]
            )
            load.start()
            loads.append(load)
    for i in range(PIECES):
        for j in range(count):
            loads[count * i + j].wait()
            for g in range(i * some, (i + 1) * some):
                out[g, j * rows : (j + 1) * rows, :] = blocks[j][:, g * lanes : (g + 1) * lanes]
        at = slice(i * some, (i + 1) * some)
        store = pltpu.make_async_copy(out.at[at], out_ref.at[at], out_sem.at[i])
        store.start()
        stores.append(store)
    for store in stores:
        store.wait()


def columns_kernel(own_ref, other_ref, start_ref, start_other_ref, out_ref):
    out_ref[...] = dot(own_ref[...], start_ref[...]) + dot(other_ref[...], start_other_ref[...])


def sum_kernel(in_ref, out_ref, *, rows):
    for at in range(0, rows, SUB):
        tiles = [in_ref[i + at : i + at + SUB, :] for i in range(0, in_ref.shape[0], rows)]
        while len(tiles) > 1:
            tiles = [a + b for a, b in zip(tiles[::2], tiles[1::2])]
        for i in range(0, out_ref.shape[0], rows):
            out_ref[i + at : i + at + SUB, :] = tiles[0]


def across_kernel(own_ref, other_ref, c_ref, x_ref, out_ref, unused_ref):
    c = c_ref[...]
    c = c * inverse_or_zero(largest(c))
    x_ref[:LANE, :] = dot(own_ref[...], c, 0, 0)
    x_ref[LANE:, :] = dot(other_ref[...], c, 0, 0)
    out_ref[...] = c


def image_kernel(own_ref, other_ref, t_ref, x_ref, x_other_ref, out_ref):
    core = lax.axis_index("core")

    @pl.when(core == 0)
    def _():
        x = x_ref[...]
        out_ref[...] = dot(own_ref[...], x[:LANE]) + dot(other_ref[...], x[LANE:])

    @pl.when(core == 1)
    def _():
        x = x_other_ref[...]
        rows = t_ref.shape[1] // 2
        first = t_ref[:, :rows, :].reshape(out_ref.shape)
        second = t_ref[:, rows:, :].reshape(out_ref.shape)
        out_ref[...] = dot(first, x[:LANE]) + dot(second, x[LANE:])


def inverse_factors(matrices):
    size = matrices[0].shape[0]
    blocks = size // SUB
    lane = lax.broadcasted_iota(jnp.int32, (SUB, size), 1)
    sub = lax.broadcasted_iota(jnp.int32, (SUB, size), 0)
    work = [[m[SUB * i : SUB * (i + 1), :] for i in range(blocks)] for m in matrices]

    def columns(rows, low):
        return [
            jnp.broadcast_to(rows[:, low + j : low + j + 1], (SUB, size)) for j in range(SUB)
        ]

    def row(values, j):
        return jnp.broadcast_to(values[j : j + 1, :], (SUB, size))

    for k in range(blocks):
        low = SUB * k
        inside = (lane >= low) & (lane < low + SUB)
        done = []
        for mine in work:
            column = columns(mine[k], low)
            w = jnp.where(inside, (lane == sub + low).astype(jnp.float32), mine[k])
            steps, pivots = [], jnp.ones((SUB, size), jnp.float32)
            for j in range(SUB):
                pivot = row(column[j], j)
                inverse = 1.0 / pivot
                pivots = jnp.where(sub == j, pivot, pivots)
                factor = jnp.where(sub > j, column[j] * inverse, 0.0)
                ahead = {}
                for i in range(j + 1, SUB):
                    ahead[i] = row(column[i], j)
                    column[i] = column[i] - factor * ahead[i]
                reduced = row(w, j)
                w = w - factor * reduced
                steps.append((inverse, ahead, reduced))
            root = lax.rsqrt(pivots)
            root = root * (1.5 - 0.5 * pivots * root * root)
            mine[k] = jnp.where(lane <= sub + low, w * root, 0.0)
            done.append(steps)
        for mine, steps in zip(work, done):
            for i in range(k + 1, blocks):
                column = columns(mine[i], low)
                w = jnp.where(inside, 0.0, mine[i])
                for j, (inverse, ahead, reduced) in enumerate(steps):
                    factor = column[j] * inverse
                    for n in range(j + 1, SUB):
                        column[n] = column[n] - factor * ahead[n]
                    w = w - factor * reduced
                mine[i] = w
    return [jnp.concatenate(mine, axis=0) for mine in work]


def final_kernel(own_ref, other_ref, c_ref, c_other_ref, basis_ref, operator_ref, y_ref):
    first = lax.axis_index("core") == 0
    y = jnp.where(first, own_ref[...], other_ref[...])
    z = jnp.where(first, other_ref[...], own_ref[...])
    c = jnp.where(first, c_ref[...], c_other_ref[...])
    scale = largest(y)
    y = y * inverse_or_zero(scale)
    y_ref[...] = y
    lower, lower_w = inverse_factors([dot(y, y, 0, 0), dot(c, y, 0, 0)])
    cross = dot(y, z, 0, 0)
    rows, total = basis_ref.shape[0], y_ref.shape[0]
    place = lax.axis_index("x") * lax.axis_size("z") + lax.axis_index("z")
    mine = y_ref[pl.ds(pl.multiple_of(place * rows, rows), rows), :]
    basis_ref[...] = dot(mine * jnp.sqrt(jnp.float32(total)), lower, 1, 1)
    operator_ref[...] = dot(dot(lower, cross), lower_w, 1, 1) * lax.rsqrt(scale)


def exchanged_rows(values, axis):
    count = lax.axis_size(axis)
    return exchanged(values.reshape(count, -1, LANE), axis).reshape(values.shape)


def summed_over_chips(part, name):
    rows = part.shape[0] // lax.axis_size(PLANE)
    kernel = functools.partial(sum_kernel, rows=rows)
    line = (lax.axis_size("z") * rows, LANE)
    (copies,) = call(kernel, name + "_plane", [line], [exchanged_rows(part, PLANE)])
    (copies,) = call(kernel, name + "_line", [part.shape], [exchanged_rows(copies, "z")])
    return exchanged_rows(copies, PLANE)


def split(name, *sources):
    rows, cols = sources[0].shape
    shape = (lax.axis_size(ROWS), len(sources) * rows, LANE)
    scratch = [pltpu.VMEM((rows, cols), jnp.float32)] * len(sources) + [
        pltpu.VMEM(shape, jnp.float32),
        pltpu.SemaphoreType.DMA((len(sources) * PIECES,)),
        pltpu.SemaphoreType.DMA((PIECES,)),
    ]
    return call(split_kernel, name, [shape], sources, scratch, pl.ANY)[0]


def on_device(hankel, shifted, start_basis):
    groups, rows_dev = lax.axis_size(ROWS), hankel.shape[0]
    rows = groups * rows_dev
    start_other = from_other_core(start_basis)
    shifted_other = to_second(shifted)
    pieces, start_other = lax.optimization_barrier((split("split", hankel), start_other))
    own = exchanged(pieces, ROWS).reshape(rows, LANE)
    other = from_other_core(own)
    both = (groups, 2 * rows_dev, LANE)

    def project(own, other, start_basis, start_other, shifted, shifted_other):
        (c_part,) = call(
            columns_kernel, "columns", [(rows, LANE)], [own, other, start_basis, start_other]
        )
        c = summed_over_chips(c_part, "columns")
        shapes = [(2 * LANE, LANE), (rows, LANE), both]
        return tuple(call(across_kernel, "across", shapes, [own, other, c]))

    def relay(own, other, start_basis, start_other, shifted, shifted_other):
        t = exchanged(split("split_shifted", shifted_other, shifted), ROWS)
        return jnp.zeros((2 * LANE, LANE), jnp.float32), jnp.zeros((rows, LANE), jnp.float32), t

    x, c, t = lax.cond(
        lax.axis_index("core") == 0, project, relay,
        own, other, start_basis, start_other, shifted, shifted_other,
    )
    x_other, c_other = from_other_core(x), to_second(c)
    (part,) = call(image_kernel, "image", [(rows, LANE)], [own, other, t, x, x_other])
    part = summed_over_chips(part, "image")
    return call(
        final_kernel,
        "factors",
        [(rows_dev, LANE), (LANE, LANE)],
        [part, from_other_core(part), c, c_other],
        [pltpu.VMEM((rows, LANE), jnp.float32)],
    )


def solution(mesh):
    finer = Mesh(mesh.devices.reshape(4, 8, 4, 2), ("x", "z", "y", "core"))
    placed = (P(ROWS, COLS), P(ROWS, COLS), P((*COLS, *ROWS), None))

    def whole(*blocks):
        return tuple(on_device(*blocks))

    return jax.shard_map(
        whole, mesh=finer, in_specs=placed, out_specs=(P(ROWS, None), P()), check_vma=False
    )
```

```python
import functools

import jax
import jax.numpy as jnp
from jax import lax
from jax.experimental import pallas as pl
from jax.experimental.pallas import tpu as pltpu
from jax.sharding import Mesh
from jax.sharding import PartitionSpec as P

ROWS = ("x", "z")
COLS = ("y", "core")
PLANE = ("x", "y")
SUB, LANE = 8, 128
PIECES = 4


def exchanged(blocks, axis):
    return lax.all_to_all(blocks, axis, 0, 0, tiled=True)


def from_other_core(value):
    return lax.ppermute(value, "core", [(0, 1), (1, 0)])


def to_second(value):
    return lax.ppermute(value, "core", [(0, 1)])


def call(kernel, name, shapes, arrays, scratch=(), space=pltpu.VMEM):
    return pl.pallas_call(
        kernel,
        name=name,
        out_shape=[jax.ShapeDtypeStruct(shape, jnp.float32) for shape in shapes],
        in_specs=[pl.BlockSpec(memory_space=space)] * len(arrays),
        out_specs=[pl.BlockSpec(memory_space=space)] * len(shapes),
        scratch_shapes=scratch,
        compiler_params=pltpu.CompilerParams(vmem_limit_bytes=(24 if space is pltpu.VMEM else 60) << 20),
    )(*arrays)


def dot(left, right, left_dim=1, right_dim=0):
    return lax.dot_general(
        left,
        right,
        (((left_dim,), (right_dim,)), ((), ())),
        precision=lax.Precision.HIGHEST,
        preferred_element_type=jnp.float32,
    )


def inverse_or_zero(scale):
    return jnp.where(scale > 0, 1.0 / jnp.where(scale > 0, scale, 1.0), 0.0)


def largest(value):
    return jnp.max(jnp.max(jnp.abs(value), axis=0, keepdims=True), axis=1, keepdims=True)


def split_kernel(*refs):
    count = (len(refs) - 4) // 2
    sources, out_ref = refs[:count], refs[count]
    blocks, out, in_sem, out_sem = refs[count + 1 : 2 * count + 1], *refs[2 * count + 1 :]
    groups, _, lanes = out.shape
    some, rows = groups // PIECES, out.shape[1] // count
    loads, stores = [], []
    for i in range(PIECES):
        at = slice(i * some * lanes, (i + 1) * some * lanes)
        for j in range(count):
            load = pltpu.make_async_copy(
                sources[j].at[:, at], blocks[j].at[:, at], in_sem.at[count * i + j]
            )
            load.start()
            loads.append(load)
    for i in range(PIECES):
        for j in range(count):
            loads[count * i + j].wait()
            for g in range(i * some, (i + 1) * some):
                out[g, j * rows : (j + 1) * rows, :] = blocks[j][:, g * lanes : (g + 1) * lanes]
        at = slice(i * some, (i + 1) * some)
        store = pltpu.make_async_copy(out.at[at], out_ref.at[at], out_sem.at[i])
        store.start()
        stores.append(store)
    for store in stores:
        store.wait()


def columns_kernel(own_ref, other_ref, start_ref, start_other_ref, out_ref):
    out_ref[...] = dot(own_ref[...], start_ref[...]) + dot(other_ref[...], start_other_ref[...])


def sum_kernel(in_ref, out_ref, *, rows):
    for at in range(0, rows, SUB):
        tiles = [in_ref[i + at : i + at + SUB, :] for i in range(0, in_ref.shape[0], rows)]
        while len(tiles) > 1:
            tiles = [a + b for a, b in zip(tiles[::2], tiles[1::2])]
        for i in range(0, out_ref.shape[0], rows):
            out_ref[i + at : i + at + SUB, :] = tiles[0]


def across_kernel(own_ref, other_ref, c_ref, x_ref, out_ref, unused_ref):
    c = c_ref[...]
    c = c * inverse_or_zero(largest(c))
    x_ref[:LANE, :] = dot(own_ref[...], c, 0, 0)
    x_ref[LANE:, :] = dot(other_ref[...], c, 0, 0)
    out_ref[...] = c


def image_kernel(own_ref, other_ref, x_ref, out_ref):
    @pl.when(lax.axis_index("core") == 0)
    def _():
        x = x_ref[...]
        out_ref[...] = dot(own_ref[...], x[:LANE]) + dot(other_ref[...], x[LANE:])


def second_image_kernel(t_ref, x_ref, image_ref, out_ref):
    core = lax.axis_index("core")

    @pl.when(core == 0)
    def _():
        out_ref[...] = image_ref[...]

    @pl.when(core == 1)
    def _():
        x = x_ref[...]
        rows = t_ref.shape[1] // 2
        first = t_ref[:, :rows, :].reshape(out_ref.shape)
        second = t_ref[:, rows:, :].reshape(out_ref.shape)
        out_ref[...] = dot(first, x[:LANE]) + dot(second, x[LANE:])


def inverse_factors(matrices):
    size = matrices[0].shape[0]
    blocks = size // SUB
    lane = lax.broadcasted_iota(jnp.int32, (SUB, size), 1)
    sub = lax.broadcasted_iota(jnp.int32, (SUB, size), 0)
    work = [[m[SUB * i : SUB * (i + 1), :] for i in range(blocks)] for m in matrices]

    def columns(rows, low):
        return [
            jnp.broadcast_to(rows[:, low + j : low + j + 1], (SUB, size)) for j in range(SUB)
        ]

    def row(values, j):
        return jnp.broadcast_to(values[j : j + 1, :], (SUB, size))

    for k in range(blocks):
        low = SUB * k
        inside = (lane >= low) & (lane < low + SUB)
        done = []
        for mine in work:
            column = columns(mine[k], low)
            w = jnp.where(inside, (lane == sub + low).astype(jnp.float32), mine[k])
            steps, pivots = [], jnp.ones((SUB, size), jnp.float32)
            for j in range(SUB):
                pivot = row(column[j], j)
                inverse = 1.0 / pivot
                pivots = jnp.where(sub == j, pivot, pivots)
                factor = jnp.where(sub > j, column[j] * inverse, 0.0)
                ahead = {}
                for i in range(j + 1, SUB):
                    ahead[i] = row(column[i], j)
                    column[i] = column[i] - factor * ahead[i]
                reduced = row(w, j)
                w = w - factor * reduced
                steps.append((inverse, ahead, reduced))
            root = lax.rsqrt(pivots)
            root = root * (1.5 - 0.5 * pivots * root * root)
            mine[k] = jnp.where(lane <= sub + low, w * root, 0.0)
            done.append(steps)
        for mine, steps in zip(work, done):
            for i in range(k + 1, blocks):
                column = columns(mine[i], low)
                w = jnp.where(inside, 0.0, mine[i])
                for j, (inverse, ahead, reduced) in enumerate(steps):
                    factor = column[j] * inverse
                    for n in range(j + 1, SUB):
                        column[n] = column[n] - factor * ahead[n]
                    w = w - factor * reduced
                mine[i] = w
    return [jnp.concatenate(mine, axis=0) for mine in work]


def factor_kernel(y_ref, c_ref, out_ref):
    @pl.when(lax.axis_index("core") == 0)
    def _():
        y = y_ref[...]
        scale = largest(y)
        y = y * inverse_or_zero(scale)
        lower, lower_w = inverse_factors([dot(y, y, 0, 0), dot(c_ref[...], y, 0, 0)])
        out_ref[:LANE, :] = lower
        out_ref[LANE : 2 * LANE, :] = lower_w
        out_ref[2 * LANE :, :] = jnp.broadcast_to(scale, (SUB, LANE))


def cross_kernel(own_ref, other_ref, after_ref, out_ref):
    first = lax.axis_index("core") == 0
    y = jnp.where(first, own_ref[...], other_ref[...])
    z = jnp.where(first, other_ref[...], own_ref[...])
    out_ref[...] = dot(y * inverse_or_zero(largest(y)), z, 0, 0)


def final_kernel(own_ref, other_ref, l_ref, l_other_ref, cross_ref, basis_ref, operator_ref):
    first = lax.axis_index("core") == 0
    factors = jnp.where(first, l_ref[...], l_other_ref[...])
    lower, lower_w = factors[:LANE], factors[LANE : 2 * LANE]
    scale = factors[2 * LANE : 2 * LANE + 1]
    rows, total = basis_ref.shape[0], own_ref.shape[0]
    place = lax.axis_index("x") * lax.axis_size("z") + lax.axis_index("z")
    at = pl.ds(pl.multiple_of(place * rows, rows), rows)
    mine = jnp.where(first, own_ref[at, :], other_ref[at, :]) * inverse_or_zero(scale)
    basis_ref[...] = dot(mine * jnp.sqrt(jnp.float32(total)), lower, 1, 1)
    operator_ref[...] = dot(dot(lower, cross_ref[...]), lower_w, 1, 1) * lax.rsqrt(scale)


def exchanged_rows(values, axis):
    count = lax.axis_size(axis)
    return exchanged(values.reshape(count, -1, LANE), axis).reshape(values.shape)


def summed_over_chips(part, name):
    rows = part.shape[0] // lax.axis_size(PLANE)
    kernel = functools.partial(sum_kernel, rows=rows)
    line = (lax.axis_size("z") * rows, LANE)
    (copies,) = call(kernel, name + "_plane", [line], [exchanged_rows(part, PLANE)])
    (copies,) = call(kernel, name + "_line", [part.shape], [exchanged_rows(copies, "z")])
    return exchanged_rows(copies, PLANE)


def split(name, *sources):
    rows, cols = sources[0].shape
    shape = (lax.axis_size(ROWS), len(sources) * rows, LANE)
    scratch = [pltpu.VMEM((rows, cols), jnp.float32)] * len(sources) + [
        pltpu.VMEM(shape, jnp.float32),
        pltpu.SemaphoreType.DMA((len(sources) * PIECES,)),
        pltpu.SemaphoreType.DMA((PIECES,)),
    ]
    return call(split_kernel, name, [shape], sources, scratch, pl.ANY)[0]


def on_device(hankel, shifted, start_basis):
    groups, rows_dev = lax.axis_size(ROWS), hankel.shape[0]
    rows = groups * rows_dev
    start_other = from_other_core(start_basis)
    shifted_other = to_second(shifted)
    pieces, start_other = lax.optimization_barrier((split("split", hankel), start_other))
    own = exchanged(pieces, ROWS).reshape(rows, LANE)
    other = from_other_core(own)
    both = (groups, 2 * rows_dev, LANE)

    def project(own, other, start_basis, start_other, shifted, shifted_other):
        (c_part,) = call(
            columns_kernel, "columns", [(rows, LANE)], [own, other, start_basis, start_other]
        )
        c = summed_over_chips(c_part, "columns")
        shapes = [(2 * LANE, LANE), (rows, LANE), both]
        return tuple(call(across_kernel, "across", shapes, [own, other, c]))

    def relay(own, other, start_basis, start_other, shifted, shifted_other):
        t = exchanged(split("split_shifted", shifted_other, shifted), ROWS)
        return jnp.zeros((2 * LANE, LANE), jnp.float32), jnp.zeros((rows, LANE), jnp.float32), t

    x, c, t = lax.cond(
        lax.axis_index("core") == 0, project, relay,
        own, other, start_basis, start_other, shifted, shifted_other,
    )
    x_other = from_other_core(x)
    (part,) = call(image_kernel, "image", [(rows, LANE)], [own, other, x])
    (part,) = call(second_image_kernel, "second_image", [(rows, LANE)], [t, x_other, part])
    part = summed_over_chips(part, "image")
    part_other = from_other_core(part)
    (factors,) = call(factor_kernel, "factors", [(2 * LANE + SUB, LANE)], [part, c])
    (cross,) = call(cross_kernel, "cross", [(LANE, LANE)], [part, part_other, factors])
    return call(
        final_kernel,
        "results",
        [(rows_dev, LANE), (LANE, LANE)],
        [part, part_other, factors, from_other_core(factors), cross],
    )


def solution(mesh):
    finer = Mesh(mesh.devices.reshape(4, 8, 4, 2), ("x", "z", "y", "core"))
    placed = (P(ROWS, COLS), P(ROWS, COLS), P((*COLS, *ROWS), None))

    def whole(*blocks):
        return tuple(on_device(*blocks))

    return jax.shard_map(
        whole, mesh=finer, in_specs=placed, out_specs=(P(ROWS, None), P()), check_vma=False
    )
```

```python
import functools

import jax
import jax.numpy as jnp
from jax import lax
from jax.experimental import pallas as pl
from jax.experimental.pallas import tpu as pltpu
from jax.sharding import Mesh
from jax.sharding import PartitionSpec as P

ROWS = ("x", "z")
COLS = ("y", "core")
PLANE = ("x", "y")
SUB, LANE = 8, 128
PIECES = 4


def exchanged(blocks, axis):
    return lax.all_to_all(blocks, axis, 0, 0, tiled=True)


def from_other_core(value):
    return lax.ppermute(value, "core", [(0, 1), (1, 0)])


def to_second(value):
    return lax.ppermute(value, "core", [(0, 1)])


def call(kernel, name, shapes, arrays, scratch=(), space=pltpu.VMEM):
    return pl.pallas_call(
        kernel,
        name=name,
        out_shape=[jax.ShapeDtypeStruct(shape, jnp.float32) for shape in shapes],
        in_specs=[pl.BlockSpec(memory_space=space)] * len(arrays),
        out_specs=[pl.BlockSpec(memory_space=space)] * len(shapes),
        scratch_shapes=scratch,
        compiler_params=pltpu.CompilerParams(vmem_limit_bytes=(24 if space is pltpu.VMEM else 60) << 20),
    )(*arrays)


def dot(left, right, left_dim=1, right_dim=0):
    return lax.dot_general(
        left,
        right,
        (((left_dim,), (right_dim,)), ((), ())),
        precision=lax.Precision.HIGHEST,
        preferred_element_type=jnp.float32,
    )


def inverse_or_zero(scale):
    return jnp.where(scale > 0, 1.0 / jnp.where(scale > 0, scale, 1.0), 0.0)


def largest(value):
    return jnp.max(jnp.max(jnp.abs(value), axis=0, keepdims=True), axis=1, keepdims=True)


def split_kernel(*refs):
    count = (len(refs) - 4) // 2
    sources, out_ref = refs[:count], refs[count]
    blocks, out, in_sem, out_sem = refs[count + 1 : 2 * count + 1], *refs[2 * count + 1 :]
    groups, _, lanes = out.shape
    some, rows = groups // PIECES, out.shape[1] // count
    loads, stores = [], []
    for i in range(PIECES):
        at = slice(i * some * lanes, (i + 1) * some * lanes)
        for j in range(count):
            load = pltpu.make_async_copy(
                sources[j].at[:, at], blocks[j].at[:, at], in_sem.at[count * i + j]
            )
            load.start()
            loads.append(load)
    for i in range(PIECES):
        for j in range(count):
            loads[count * i + j].wait()
            for g in range(i * some, (i + 1) * some):
                out[g, j * rows : (j + 1) * rows, :] = blocks[j][:, g * lanes : (g + 1) * lanes]
        at = slice(i * some, (i + 1) * some)
        store = pltpu.make_async_copy(out.at[at], out_ref.at[at], out_sem.at[i])
        store.start()
        stores.append(store)
    for store in stores:
        store.wait()


def beside(left, right):
    return jnp.concatenate([left, right], axis=1)


def columns_kernel(own_ref, other_ref, start_ref, start_other_ref, out_ref):
    start = jnp.concatenate([start_ref[...], start_other_ref[...]])
    out_ref[...] = dot(beside(own_ref[...], other_ref[...]), start)


def sum_kernel(in_ref, out_ref, *, rows):
    for at in range(0, rows, SUB):
        tiles = [in_ref[i + at : i + at + SUB, :] for i in range(0, in_ref.shape[0], rows)]
        while len(tiles) > 1:
            tiles = [a + b for a, b in zip(tiles[::2], tiles[1::2])]
        for i in range(0, out_ref.shape[0], rows):
            out_ref[i + at : i + at + SUB, :] = tiles[0]


def across_kernel(own_ref, other_ref, c_ref, x_ref, out_ref, unused_ref):
    c = c_ref[...]
    c = c * inverse_or_zero(largest(c))
    x_ref[...] = dot(c, beside(own_ref[...], other_ref[...]), 0, 0)
    out_ref[...] = c


def image_kernel(own_ref, other_ref, x_ref, out_ref):
    @pl.when(lax.axis_index("core") == 0)
    def _():
        out_ref[...] = dot(beside(own_ref[...], other_ref[...]), x_ref[...], 1, 1)


def second_image_kernel(t_ref, x_ref, image_ref, out_ref):
    core = lax.axis_index("core")

    @pl.when(core == 0)
    def _():
        out_ref[...] = image_ref[...]

    @pl.when(core == 1)
    def _():
        rows = t_ref.shape[1] // 2
        first = t_ref[:, :rows, :].reshape(out_ref.shape)
        second = t_ref[:, rows:, :].reshape(out_ref.shape)
        out_ref[...] = dot(beside(first, second), x_ref[...], 1, 1)


def inverse_factors(matrices):
    size = matrices[0].shape[0]
    blocks = size // SUB
    lane = lax.broadcasted_iota(jnp.int32, (SUB, size), 1)
    sub = lax.broadcasted_iota(jnp.int32, (SUB, size), 0)
    work = [[m[SUB * i : SUB * (i + 1), :] for i in range(blocks)] for m in matrices]

    def columns(rows, low):
        return [
            jnp.broadcast_to(rows[:, low + j : low + j + 1], (SUB, size)) for j in range(SUB)
        ]

    def row(values, j):
        return jnp.broadcast_to(values[j : j + 1, :], (SUB, size))

    for k in range(blocks):
        low = SUB * k
        inside = (lane >= low) & (lane < low + SUB)
        done = []
        for mine in work:
            column = columns(mine[k], low)
            w = jnp.where(inside, (lane == sub + low).astype(jnp.float32), mine[k])
            steps, pivots = [], jnp.ones((SUB, size), jnp.float32)
            for j in range(SUB):
                pivot = row(column[j], j)
                inverse = 1.0 / pivot
                pivots = jnp.where(sub == j, pivot, pivots)
                factor = jnp.where(sub > j, column[j] * inverse, 0.0)
                ahead = {}
                for i in range(j + 1, SUB):
                    ahead[i] = row(column[i], j)
                    column[i] = column[i] - factor * ahead[i]
                reduced = row(w, j)
                w = w - factor * reduced
                steps.append((inverse, ahead, reduced))
            root = lax.rsqrt(pivots)
            root = root * (1.5 - 0.5 * pivots * root * root)
            mine[k] = jnp.where(lane <= sub + low, w * root, 0.0)
            done.append(steps)
        for mine, steps in zip(work, done):
            for i in range(k + 1, blocks):
                column = columns(mine[i], low)
                w = jnp.where(inside, 0.0, mine[i])
                for j, (inverse, ahead, reduced) in enumerate(steps):
                    factor = column[j] * inverse
                    for n in range(j + 1, SUB):
                        column[n] = column[n] - factor * ahead[n]
                    w = w - factor * reduced
                mine[i] = w
    return [jnp.concatenate(mine, axis=0) for mine in work]


def factor_kernel(y_ref, c_ref, out_ref):
    @pl.when(lax.axis_index("core") == 0)
    def _():
        y = y_ref[...]
        scale = largest(y)
        y = y * inverse_or_zero(scale)
        grams = dot(y, beside(y, c_ref[...]), 0, 0)
        lower, lower_w = inverse_factors([grams[:, :LANE], grams[:, LANE:]])
        out_ref[:LANE, :] = lower
        out_ref[LANE : 2 * LANE, :] = lower_w
        out_ref[2 * LANE :, :] = jnp.broadcast_to(scale, (SUB, LANE))


def cross_kernel(own_ref, other_ref, after_ref, out_ref):
    first = lax.axis_index("core") == 0
    y = jnp.where(first, own_ref[...], other_ref[...])
    z = jnp.where(first, other_ref[...], own_ref[...])
    out_ref[...] = dot(y * inverse_or_zero(largest(y)), z, 0, 0)


def final_kernel(own_ref, other_ref, l_ref, l_other_ref, cross_ref, basis_ref, operator_ref):
    first = lax.axis_index("core") == 0
    factors = jnp.where(first, l_ref[...], l_other_ref[...])
    lower, lower_w = factors[:LANE], factors[LANE : 2 * LANE]
    scale = factors[2 * LANE : 2 * LANE + 1]
    rows, total = basis_ref.shape[0], own_ref.shape[0]
    place = lax.axis_index("x") * lax.axis_size("z") + lax.axis_index("z")
    at = pl.ds(pl.multiple_of(place * rows, rows), rows)
    mine = jnp.where(first, own_ref[at, :], other_ref[at, :]) * inverse_or_zero(scale)
    basis_ref[...] = dot(mine * jnp.sqrt(jnp.float32(total)), lower, 1, 1)
    operator_ref[...] = dot(dot(lower, cross_ref[...]), lower_w, 1, 1) * lax.rsqrt(scale)


def exchanged_rows(values, axis):
    count = lax.axis_size(axis)
    return exchanged(values.reshape(count, -1, LANE), axis).reshape(values.shape)


def summed_over_chips(part, name):
    rows = part.shape[0] // lax.axis_size(PLANE)
    kernel = functools.partial(sum_kernel, rows=rows)
    line = (lax.axis_size("z") * rows, LANE)
    (copies,) = call(kernel, name + "_plane", [line], [exchanged_rows(part, PLANE)])
    (copies,) = call(kernel, name + "_line", [part.shape], [exchanged_rows(copies, "z")])
    return exchanged_rows(copies, PLANE)


def split(name, *sources):
    rows, cols = sources[0].shape
    shape = (lax.axis_size(ROWS), len(sources) * rows, LANE)
    scratch = [pltpu.VMEM((rows, cols), jnp.float32)] * len(sources) + [
        pltpu.VMEM(shape, jnp.float32),
        pltpu.SemaphoreType.DMA((len(sources) * PIECES,)),
        pltpu.SemaphoreType.DMA((PIECES,)),
    ]
    return call(split_kernel, name, [shape], sources, scratch, pl.ANY)[0]


def on_device(hankel, shifted, start_basis):
    groups, rows_dev = lax.axis_size(ROWS), hankel.shape[0]
    rows = groups * rows_dev
    start_other = from_other_core(start_basis)
    shifted_other = to_second(shifted)
    pieces, start_other = lax.optimization_barrier((split("split", hankel), start_other))
    own = exchanged(pieces, ROWS).reshape(rows, LANE)
    other = from_other_core(own)
    both = (groups, 2 * rows_dev, LANE)

    def project(own, other, start_basis, start_other, shifted, shifted_other):
        (c_part,) = call(
            columns_kernel, "columns", [(rows, LANE)], [own, other, start_basis, start_other]
        )
        c = summed_over_chips(c_part, "columns")
        shapes = [(LANE, 2 * LANE), (rows, LANE), both]
        return tuple(call(across_kernel, "across", shapes, [own, other, c]))

    def relay(own, other, start_basis, start_other, shifted, shifted_other):
        t = exchanged(split("split_shifted", shifted_other, shifted), ROWS)
        return jnp.zeros((LANE, 2 * LANE), jnp.float32), jnp.zeros((rows, LANE), jnp.float32), t

    x, c, t = lax.cond(
        lax.axis_index("core") == 0, project, relay,
        own, other, start_basis, start_other, shifted, shifted_other,
    )
    x_other = from_other_core(x)
    (part,) = call(image_kernel, "image", [(rows, LANE)], [own, other, x])
    (part,) = call(second_image_kernel, "second_image", [(rows, LANE)], [t, x_other, part])
    part = summed_over_chips(part, "image")
    part_other = from_other_core(part)
    (factors,) = call(factor_kernel, "factors", [(2 * LANE + SUB, LANE)], [part, c])
    (cross,) = call(cross_kernel, "cross", [(LANE, LANE)], [part, part_other, factors])
    return call(
        final_kernel,
        "results",
        [(rows_dev, LANE), (LANE, LANE)],
        [part, part_other, factors, from_other_core(factors), cross],
    )


def solution(mesh):
    finer = Mesh(mesh.devices.reshape(4, 8, 4, 2), ("x", "z", "y", "core"))
    placed = (P(ROWS, COLS), P(ROWS, COLS), P((*COLS, *ROWS), None))

    def whole(*blocks):
        return tuple(on_device(*blocks))

    return jax.shard_map(
        whole, mesh=finer, in_specs=placed, out_specs=(P(ROWS, None), P()), check_vma=False
    )
```

```python
import functools

import jax
import jax.numpy as jnp
from jax import lax
from jax.experimental import pallas as pl
from jax.experimental.pallas import tpu as pltpu
from jax.sharding import Mesh
from jax.sharding import PartitionSpec as P

ROWS = ("x", "z")
COLS = ("y", "core")
PLANE = ("x", "y")
SUB, LANE = 8, 128
PIECES = 4


def exchanged(blocks, axis):
    return lax.all_to_all(blocks, axis, 0, 0, tiled=True)


def from_other_core(value):
    return lax.ppermute(value, "core", [(0, 1), (1, 0)])


def to_second(value):
    return lax.ppermute(value, "core", [(0, 1)])


def call(kernel, name, shapes, arrays, scratch=(), space=pltpu.VMEM):
    return pl.pallas_call(
        kernel,
        name=name,
        out_shape=[jax.ShapeDtypeStruct(shape, jnp.float32) for shape in shapes],
        in_specs=[pl.BlockSpec(memory_space=space)] * len(arrays),
        out_specs=[pl.BlockSpec(memory_space=space)] * len(shapes),
        scratch_shapes=scratch,
        compiler_params=pltpu.CompilerParams(vmem_limit_bytes=(24 if space is pltpu.VMEM else 60) << 20),
    )(*arrays)


def dot(left, right, left_dim=1, right_dim=0):
    return lax.dot_general(
        left,
        right,
        (((left_dim,), (right_dim,)), ((), ())),
        precision=lax.Precision.HIGHEST,
        preferred_element_type=jnp.float32,
    )


def inverse_or_zero(scale):
    return jnp.where(scale > 0, 1.0 / jnp.where(scale > 0, scale, 1.0), 0.0)


def largest(value):
    return jnp.max(jnp.max(jnp.abs(value), axis=0, keepdims=True), axis=1, keepdims=True)


def split_kernel(*refs):
    count = (len(refs) - 4) // 2
    sources, out_ref = refs[:count], refs[count]
    blocks, out, in_sem, out_sem = refs[count + 1 : 2 * count + 1], *refs[2 * count + 1 :]
    groups, _, lanes = out.shape
    some, rows = groups // PIECES, out.shape[1] // count
    loads, stores = [], []
    for i in range(PIECES):
        at = slice(i * some * lanes, (i + 1) * some * lanes)
        for j in range(count):
            load = pltpu.make_async_copy(
                sources[j].at[:, at], blocks[j].at[:, at], in_sem.at[count * i + j]
            )
            load.start()
            loads.append(load)
    for i in range(PIECES):
        for j in range(count):
            loads[count * i + j].wait()
            for g in range(i * some, (i + 1) * some):
                out[g, j * rows : (j + 1) * rows, :] = blocks[j][:, g * lanes : (g + 1) * lanes]
        at = slice(i * some, (i + 1) * some)
        store = pltpu.make_async_copy(out.at[at], out_ref.at[at], out_sem.at[i])
        store.start()
        stores.append(store)
    for store in stores:
        store.wait()


def beside(left, right):
    return jnp.concatenate([left, right], axis=1)


def first_columns_kernel(own_ref, start_ref, out_ref):
    out_ref[...] = dot(own_ref[...], start_ref[...])


def columns_kernel(other_ref, start_ref, columns_ref, out_ref):
    out_ref[...] = columns_ref[...] + dot(other_ref[...], start_ref[...])


def sum_kernel(in_ref, out_ref, *, rows):
    for at in range(0, rows, SUB):
        tiles = [in_ref[i + at : i + at + SUB, :] for i in range(0, in_ref.shape[0], rows)]
        while len(tiles) > 1:
            tiles = [a + b for a, b in zip(tiles[::2], tiles[1::2])]
        for i in range(0, out_ref.shape[0], rows):
            out_ref[i + at : i + at + SUB, :] = tiles[0]


def across_kernel(own_ref, other_ref, c_ref, x_ref, out_ref, unused_ref):
    c = c_ref[...]
    c = c * inverse_or_zero(largest(c))
    x_ref[...] = dot(c, beside(own_ref[...], other_ref[...]), 0, 0)
    out_ref[...] = c


def image_kernel(own_ref, other_ref, x_ref, out_ref):
    @pl.when(lax.axis_index("core") == 0)
    def _():
        out_ref[...] = dot(beside(own_ref[...], other_ref[...]), x_ref[...], 1, 1)


def second_image_kernel(t_ref, x_ref, image_ref, out_ref):
    core = lax.axis_index("core")

    @pl.when(core == 0)
    def _():
        out_ref[...] = image_ref[...]

    @pl.when(core == 1)
    def _():
        rows = t_ref.shape[1] // 2
        first = t_ref[:, :rows, :].reshape(out_ref.shape)
        second = t_ref[:, rows:, :].reshape(out_ref.shape)
        out_ref[...] = dot(beside(first, second), x_ref[...], 1, 1)


def inverse_factors(matrices):
    size = matrices[0].shape[0]
    blocks = size // SUB
    lane = lax.broadcasted_iota(jnp.int32, (SUB, size), 1)
    sub = lax.broadcasted_iota(jnp.int32, (SUB, size), 0)
    work = [[m[SUB * i : SUB * (i + 1), :] for i in range(blocks)] for m in matrices]

    def columns(rows, low):
        return [
            jnp.broadcast_to(rows[:, low + j : low + j + 1], (SUB, size)) for j in range(SUB)
        ]

    def row(values, j):
        return jnp.broadcast_to(values[j : j + 1, :], (SUB, size))

    for k in range(blocks):
        low = SUB * k
        inside = (lane >= low) & (lane < low + SUB)
        done = []
        for mine in work:
            column = columns(mine[k], low)
            w = jnp.where(inside, (lane == sub + low).astype(jnp.float32), mine[k])
            steps, pivots = [], jnp.ones((SUB, size), jnp.float32)
            for j in range(SUB):
                pivot = row(column[j], j)
                inverse = 1.0 / pivot
                pivots = jnp.where(sub == j, pivot, pivots)
                factor = jnp.where(sub > j, column[j] * inverse, 0.0)
                ahead = {}
                for i in range(j + 1, SUB):
                    ahead[i] = row(column[i], j)
                    column[i] = column[i] - factor * ahead[i]
                reduced = row(w, j)
                w = w - factor * reduced
                steps.append((inverse, ahead, reduced))
            root = lax.rsqrt(pivots)
            root = root * (1.5 - 0.5 * pivots * root * root)
            mine[k] = jnp.where(lane <= sub + low, w * root, 0.0)
            done.append(steps)
        for mine, steps in zip(work, done):
            for i in range(k + 1, blocks):
                column = columns(mine[i], low)
                w = jnp.where(inside, 0.0, mine[i])
                for j, (inverse, ahead, reduced) in enumerate(steps):
                    factor = column[j] * inverse
                    for n in range(j + 1, SUB):
                        column[n] = column[n] - factor * ahead[n]
                    w = w - factor * reduced
                mine[i] = w
    return [jnp.concatenate(mine, axis=0) for mine in work]


def factor_kernel(y_ref, c_ref, out_ref):
    @pl.when(lax.axis_index("core") == 0)
    def _():
        y = y_ref[...]
        scale = largest(y)
        y = y * inverse_or_zero(scale)
        grams = dot(y, beside(y, c_ref[...]), 0, 0)
        lower, lower_w = inverse_factors([grams[:, :LANE], grams[:, LANE:]])
        out_ref[:LANE, :] = lower
        out_ref[LANE : 2 * LANE, :] = lower_w
        out_ref[2 * LANE :, :] = jnp.broadcast_to(scale, (SUB, LANE))


def cross_kernel(own_ref, other_ref, after_ref, out_ref):
    first = lax.axis_index("core") == 0
    y = jnp.where(first, own_ref[...], other_ref[...])
    z = jnp.where(first, other_ref[...], own_ref[...])
    out_ref[...] = dot(y * inverse_or_zero(largest(y)), z, 0, 0)


def final_kernel(own_ref, other_ref, l_ref, l_other_ref, cross_ref, basis_ref, operator_ref):
    first = lax.axis_index("core") == 0
    factors = jnp.where(first, l_ref[...], l_other_ref[...])
    lower, lower_w = factors[:LANE], factors[LANE : 2 * LANE]
    scale = factors[2 * LANE : 2 * LANE + 1]
    rows, total = basis_ref.shape[0], own_ref.shape[0]
    place = lax.axis_index("x") * lax.axis_size("z") + lax.axis_index("z")
    at = pl.ds(pl.multiple_of(place * rows, rows), rows)
    mine = jnp.where(first, own_ref[at, :], other_ref[at, :]) * inverse_or_zero(scale)
    basis_ref[...] = dot(mine * jnp.sqrt(jnp.float32(total)), lower, 1, 1)
    operator_ref[...] = dot(dot(lower, cross_ref[...]), lower_w, 1, 1) * lax.rsqrt(scale)


def exchanged_rows(values, axis):
    count = lax.axis_size(axis)
    return exchanged(values.reshape(count, -1, LANE), axis).reshape(values.shape)


def summed_over_chips(part, name):
    rows = part.shape[0] // lax.axis_size(PLANE)
    kernel = functools.partial(sum_kernel, rows=rows)
    line = (lax.axis_size("z") * rows, LANE)
    (copies,) = call(kernel, name + "_plane", [line], [exchanged_rows(part, PLANE)])
    (copies,) = call(kernel, name + "_line", [part.shape], [exchanged_rows(copies, "z")])
    return exchanged_rows(copies, PLANE)


def split(name, *sources):
    rows, cols = sources[0].shape
    shape = (lax.axis_size(ROWS), len(sources) * rows, LANE)
    scratch = [pltpu.VMEM((rows, cols), jnp.float32)] * len(sources) + [
        pltpu.VMEM(shape, jnp.float32),
        pltpu.SemaphoreType.DMA((len(sources) * PIECES,)),
        pltpu.SemaphoreType.DMA((PIECES,)),
    ]
    return call(split_kernel, name, [shape], sources, scratch, pl.ANY)[0]


def on_device(hankel, shifted, start_basis):
    groups, rows_dev = lax.axis_size(ROWS), hankel.shape[0]
    rows = groups * rows_dev
    start_other = from_other_core(start_basis)
    shifted_other = to_second(shifted)
    pieces, start_other = lax.optimization_barrier((split("split", hankel), start_other))
    own = exchanged(pieces, ROWS).reshape(rows, LANE)
    other = from_other_core(own)
    (c_part,) = call(first_columns_kernel, "first_columns", [(rows, LANE)], [own, start_basis])
    both = (groups, 2 * rows_dev, LANE)

    def project(own, other, c_part, start_other, shifted, shifted_other):
        (c_part,) = call(columns_kernel, "columns", [(rows, LANE)], [other, start_other, c_part])
        c = summed_over_chips(c_part, "columns")
        shapes = [(LANE, 2 * LANE), (rows, LANE), both]
        return tuple(call(across_kernel, "across", shapes, [own, other, c]))

    def relay(own, other, c_part, start_other, shifted, shifted_other):
        t = exchanged(split("split_shifted", shifted_other, shifted), ROWS)
        return jnp.zeros((LANE, 2 * LANE), jnp.float32), jnp.zeros((rows, LANE), jnp.float32), t

    x, c, t = lax.cond(
        lax.axis_index("core") == 0, project, relay,
        own, other, c_part, start_other, shifted, shifted_other,
    )
    x_other = from_other_core(x)
    (part,) = call(image_kernel, "image", [(rows, LANE)], [own, other, x])
    (part,) = call(second_image_kernel, "second_image", [(rows, LANE)], [t, x_other, part])
    part = summed_over_chips(part, "image")
    part_other = from_other_core(part)
    (factors,) = call(factor_kernel, "factors", [(2 * LANE + SUB, LANE)], [part, c])
    (cross,) = call(cross_kernel, "cross", [(LANE, LANE)], [part, part_other, factors])
    return call(
        final_kernel,
        "results",
        [(rows_dev, LANE), (LANE, LANE)],
        [part, part_other, factors, from_other_core(factors), cross],
    )


def solution(mesh):
    finer = Mesh(mesh.devices.reshape(4, 8, 4, 2), ("x", "z", "y", "core"))
    placed = (P(ROWS, COLS), P(ROWS, COLS), P((*COLS, *ROWS), None))

    def whole(*blocks):
        return tuple(on_device(*blocks))

    return jax.shard_map(
        whole, mesh=finer, in_specs=placed, out_specs=(P(ROWS, None), P()), check_vma=False
    )
```

```python
import functools

import jax
import jax.numpy as jnp
from jax import lax
from jax.experimental import pallas as pl
from jax.experimental.pallas import tpu as pltpu
from jax.sharding import Mesh
from jax.sharding import PartitionSpec as P

ROWS = ("x", "z")
COLS = ("y", "core")
PLANE = ("x", "y")
SUB, LANE = 8, 128
PIECES = 4


def exchanged(blocks, axis):
    return lax.all_to_all(blocks, axis, 0, 0, tiled=True)


def from_other_core(value):
    return lax.ppermute(value, "core", [(0, 1), (1, 0)])


def call(kernel, name, shapes, arrays, scratch=(), space=pltpu.VMEM):
    return pl.pallas_call(
        kernel,
        name=name,
        out_shape=[jax.ShapeDtypeStruct(shape, jnp.float32) for shape in shapes],
        in_specs=[pl.BlockSpec(memory_space=space)] * len(arrays),
        out_specs=[pl.BlockSpec(memory_space=space)] * len(shapes),
        scratch_shapes=scratch,
        compiler_params=pltpu.CompilerParams(vmem_limit_bytes=(24 if space is pltpu.VMEM else 60) << 20),
    )(*arrays)


def dot(left, right, left_dim=1, right_dim=0):
    return lax.dot_general(
        left,
        right,
        (((left_dim,), (right_dim,)), ((), ())),
        precision=lax.Precision.HIGHEST,
        preferred_element_type=jnp.float32,
    )


def inverse_or_zero(scale):
    return jnp.where(scale > 0, 1.0 / jnp.where(scale > 0, scale, 1.0), 0.0)


def largest(value):
    return jnp.max(jnp.max(jnp.abs(value), axis=0, keepdims=True), axis=1, keepdims=True)


def split_kernel(*refs):
    count = (len(refs) - 4) // 2
    sources, out_ref = refs[:count], refs[count]
    blocks, out, in_sem, out_sem = refs[count + 1 : 2 * count + 1], *refs[2 * count + 1 :]
    groups, _, lanes = out.shape
    some, rows = groups // PIECES, out.shape[1] // count
    loads, stores = [], []
    for i in range(PIECES):
        at = slice(i * some * lanes, (i + 1) * some * lanes)
        for j in range(count):
            load = pltpu.make_async_copy(
                sources[j].at[:, at], blocks[j].at[:, at], in_sem.at[count * i + j]
            )
            load.start()
            loads.append(load)
    for i in range(PIECES):
        for j in range(count):
            loads[count * i + j].wait()
            for g in range(i * some, (i + 1) * some):
                out[g, j * rows : (j + 1) * rows, :] = blocks[j][:, g * lanes : (g + 1) * lanes]
        at = slice(i * some, (i + 1) * some)
        store = pltpu.make_async_copy(out.at[at], out_ref.at[at], out_sem.at[i])
        store.start()
        stores.append(store)
    for store in stores:
        store.wait()


def beside(left, right):
    return jnp.concatenate([left, right], axis=1)


def first_columns_kernel(own_ref, start_ref, keep_ref, send_ref):
    first = lax.axis_index("core") == 0
    columns = dot(own_ref[...], start_ref[...])
    half = keep_ref.shape[0]
    keep_ref[...] = jnp.where(first, columns[:half], columns[half:])
    send_ref[...] = jnp.where(first, columns[half:], columns[:half])


def columns_kernel(keep_ref, other_ref, out_ref):
    out_ref[...] = keep_ref[...] + other_ref[...]


def copies_kernel(own_ref, other_ref, out_ref):
    rows = own_ref.shape[0]
    for i in range(0, out_ref.shape[0], 2 * rows):
        out_ref[i : i + rows, :] = own_ref[...]
        out_ref[i + rows : i + 2 * rows, :] = other_ref[...]


def sum_kernel(in_ref, out_ref, *, rows):
    for at in range(0, rows, SUB):
        tiles = [in_ref[i + at : i + at + SUB, :] for i in range(0, in_ref.shape[0], rows)]
        while len(tiles) > 1:
            tiles = [a + b for a, b in zip(tiles[::2], tiles[1::2])]
        for i in range(0, out_ref.shape[0], rows):
            out_ref[i + at : i + at + SUB, :] = tiles[0]


def across_kernel(own_ref, other_ref, c_ref, x_ref, out_ref, unused_ref):
    c = c_ref[...].reshape(lax.axis_size(PLANE), 2, -1, LANE)
    c = jnp.concatenate([c[:, core].reshape(-1, LANE) for core in range(2)])
    c = c * inverse_or_zero(largest(c))
    x_ref[...] = dot(c, beside(own_ref[...], other_ref[...]), 0, 0)
    out_ref[...] = c


def image_kernel(own_ref, other_ref, x_ref, out_ref):
    @pl.when(lax.axis_index("core") == 0)
    def _():
        out_ref[...] = dot(beside(own_ref[...], other_ref[...]), x_ref[...], 1, 1)


def second_image_kernel(t_ref, x_ref, image_ref, out_ref):
    core = lax.axis_index("core")

    @pl.when(core == 0)
    def _():
        out_ref[...] = image_ref[...]

    @pl.when(core == 1)
    def _():
        rows = t_ref.shape[1] // 2
        first = t_ref[:, :rows, :].reshape(out_ref.shape)
        second = t_ref[:, rows:, :].reshape(out_ref.shape)
        out_ref[...] = dot(beside(first, second), x_ref[...], 1, 1)


def inverse_factors(matrices):
    size = matrices[0].shape[0]
    blocks = size // SUB
    lane = lax.broadcasted_iota(jnp.int32, (SUB, size), 1)
    sub = lax.broadcasted_iota(jnp.int32, (SUB, size), 0)
    work = [[m[SUB * i : SUB * (i + 1), :] for i in range(blocks)] for m in matrices]

    def columns(rows, low):
        return [
            jnp.broadcast_to(rows[:, low + j : low + j + 1], (SUB, size)) for j in range(SUB)
        ]

    def row(values, j):
        return jnp.broadcast_to(values[j : j + 1, :], (SUB, size))

    for k in range(blocks):
        low = SUB * k
        inside = (lane >= low) & (lane < low + SUB)
        done = []
        for mine in work:
            column = columns(mine[k], low)
            w = jnp.where(inside, (lane == sub + low).astype(jnp.float32), mine[k])
            steps, pivots = [], jnp.ones((SUB, size), jnp.float32)
            for j in range(SUB):
                pivot = row(column[j], j)
                inverse = 1.0 / pivot
                pivots = jnp.where(sub == j, pivot, pivots)
                factor = jnp.where(sub > j, column[j] * inverse, 0.0)
                ahead = {}
                for i in range(j + 1, SUB):
                    ahead[i] = row(column[i], j)
                    column[i] = column[i] - factor * ahead[i]
                reduced = row(w, j)
                w = w - factor * reduced
                steps.append((inverse, ahead, reduced))
            root = lax.rsqrt(pivots)
            root = root * (1.5 - 0.5 * pivots * root * root)
            mine[k] = jnp.where(lane <= sub + low, w * root, 0.0)
            done.append(steps)
        for mine, steps in zip(work, done):
            for i in range(k + 1, blocks):
                column = columns(mine[i], low)
                w = jnp.where(inside, 0.0, mine[i])
                for j, (inverse, ahead, reduced) in enumerate(steps):
                    factor = column[j] * inverse
                    for n in range(j + 1, SUB):
                        column[n] = column[n] - factor * ahead[n]
                    w = w - factor * reduced
                mine[i] = w
    return [jnp.concatenate(mine, axis=0) for mine in work]


def factor_kernel(y_ref, c_ref, out_ref):
    @pl.when(lax.axis_index("core") == 0)
    def _():
        y = y_ref[...]
        scale = largest(y)
        y = y * inverse_or_zero(scale)
        grams = dot(y, beside(y, c_ref[...]), 0, 0)
        lower, lower_w = inverse_factors([grams[:, :LANE], grams[:, LANE:]])
        out_ref[:LANE, :] = lower
        out_ref[LANE : 2 * LANE, :] = lower_w
        out_ref[2 * LANE :, :] = jnp.broadcast_to(scale, (SUB, LANE))


def cross_kernel(own_ref, other_ref, after_ref, out_ref):
    first = lax.axis_index("core") == 0
    y = jnp.where(first, own_ref[...], other_ref[...])
    z = jnp.where(first, other_ref[...], own_ref[...])
    out_ref[...] = dot(y * inverse_or_zero(largest(y)), z, 0, 0)


def final_kernel(own_ref, other_ref, l_ref, l_other_ref, cross_ref, basis_ref, operator_ref):
    first = lax.axis_index("core") == 0
    factors = jnp.where(first, l_ref[...], l_other_ref[...])
    lower, lower_w = factors[:LANE], factors[LANE : 2 * LANE]
    scale = factors[2 * LANE : 2 * LANE + 1]
    rows, total = basis_ref.shape[0], own_ref.shape[0]
    place = lax.axis_index("x") * lax.axis_size("z") + lax.axis_index("z")
    at = pl.ds(pl.multiple_of(place * rows, rows), rows)
    mine = jnp.where(first, own_ref[at, :], other_ref[at, :]) * inverse_or_zero(scale)
    basis_ref[...] = dot(mine * jnp.sqrt(jnp.float32(total)), lower, 1, 1)
    operator_ref[...] = dot(dot(lower, cross_ref[...]), lower_w, 1, 1) * lax.rsqrt(scale)


def exchanged_rows(values, axis):
    count = lax.axis_size(axis)
    return exchanged(values.reshape(count, -1, LANE), axis).reshape(values.shape)


def summed_pieces(part, name, pieces):
    rows = part.shape[0] // lax.axis_size(PLANE)
    kernel = functools.partial(sum_kernel, rows=rows)
    line = (lax.axis_size("z") * rows, LANE)
    (copies,) = call(kernel, name + "_plane", [line], [exchanged_rows(part, PLANE)])
    shapes = [(pieces * rows, LANE)]
    return call(kernel, name + "_line", shapes, [exchanged_rows(copies, "z")])[0]


def split(name, *sources):
    rows, cols = sources[0].shape
    shape = (lax.axis_size(ROWS), len(sources) * rows, LANE)
    scratch = [pltpu.VMEM((rows, cols), jnp.float32)] * len(sources) + [
        pltpu.VMEM(shape, jnp.float32),
        pltpu.SemaphoreType.DMA((len(sources) * PIECES,)),
        pltpu.SemaphoreType.DMA((PIECES,)),
    ]
    return call(split_kernel, name, [shape], sources, scratch, pl.ANY)[0]


def on_device(hankel, shifted, start_basis):
    groups, rows_dev = lax.axis_size(ROWS), hankel.shape[0]
    rows = groups * rows_dev
    pieces, shifted_other = lax.optimization_barrier(
        (split("split", hankel), from_other_core(shifted))
    )
    own = exchanged(pieces, ROWS).reshape(rows, LANE)
    halves = [(rows // 2, LANE)] * 2
    keep, send = call(first_columns_kernel, "first_columns", halves, [own, start_basis])
    received, own = lax.optimization_barrier((from_other_core(send), own))
    other = from_other_core(own)
    (c_part,) = call(columns_kernel, "columns", halves[:1], [keep, received])
    piece = summed_pieces(c_part, "columns", 1)
    piece_other = from_other_core(piece)
    both = (groups, 2 * rows_dev, LANE)

    def project(own, other, piece, piece_other, shifted, shifted_other):
        (copies,) = call(copies_kernel, "copies", [(rows, LANE)], [piece, piece_other])
        c = exchanged_rows(copies, PLANE)
        shapes = [(LANE, 2 * LANE), (rows, LANE), both]
        return tuple(call(across_kernel, "across", shapes, [own, other, c]))

    def relay(own, other, piece, piece_other, shifted, shifted_other):
        t = exchanged(split("split_shifted", shifted_other, shifted), ROWS)
        return jnp.zeros((LANE, 2 * LANE), jnp.float32), jnp.zeros((rows, LANE), jnp.float32), t

    x, c, t = lax.cond(
        lax.axis_index("core") == 0, project, relay,
        own, other, piece, piece_other, shifted, shifted_other,
    )
    x_other = from_other_core(x)
    (part,) = call(image_kernel, "image", [(rows, LANE)], [own, other, x])
    (part,) = call(second_image_kernel, "second_image", [(rows, LANE)], [t, x_other, part])
    part = exchanged_rows(summed_pieces(part, "image", lax.axis_size(PLANE)), PLANE)
    part_other = from_other_core(part)
    (factors,) = call(factor_kernel, "factors", [(2 * LANE + SUB, LANE)], [part, c])
    (cross,) = call(cross_kernel, "cross", [(LANE, LANE)], [part, part_other, factors])
    return call(
        final_kernel,
        "results",
        [(rows_dev, LANE), (LANE, LANE)],
        [part, part_other, factors, from_other_core(factors), cross],
    )


def solution(mesh):
    finer = Mesh(mesh.devices.reshape(4, 8, 4, 2), ("x", "z", "y", "core"))
    placed = (P(ROWS, COLS), P(ROWS, COLS), P((*COLS, *ROWS), None))

    def whole(*blocks):
        return tuple(on_device(*blocks))

    return jax.shard_map(
        whole, mesh=finer, in_specs=placed, out_specs=(P(ROWS, None), P()), check_vma=False
    )
```

```python
import functools

import jax
import jax.numpy as jnp
from jax import lax
from jax.experimental import pallas as pl
from jax.experimental.pallas import tpu as pltpu
from jax.sharding import Mesh
from jax.sharding import PartitionSpec as P

ROWS = ("x", "z")
COLS = ("y", "core")
PLANE = ("y", "x")
SUB, LANE = 8, 128
PIECES = 4


def exchanged(blocks, axis):
    return lax.all_to_all(blocks, axis, 0, 0, tiled=True)


def from_other_core(value):
    return lax.ppermute(value, "core", [(0, 1), (1, 0)])


def to_second(value):
    return lax.ppermute(value, "core", [(0, 1)])


def call(kernel, name, shapes, arrays, scratch=(), space=pltpu.VMEM):
    return pl.pallas_call(
        kernel,
        name=name,
        out_shape=[jax.ShapeDtypeStruct(shape, jnp.float32) for shape in shapes],
        in_specs=[pl.BlockSpec(memory_space=space)] * len(arrays),
        out_specs=[pl.BlockSpec(memory_space=space)] * len(shapes),
        scratch_shapes=scratch,
        compiler_params=pltpu.CompilerParams(vmem_limit_bytes=(24 if space is pltpu.VMEM else 60) << 20),
    )(*arrays)


def dot(left, right, left_dim=1, right_dim=0):
    return lax.dot_general(
        left,
        right,
        (((left_dim,), (right_dim,)), ((), ())),
        precision=lax.Precision.HIGHEST,
        preferred_element_type=jnp.float32,
    )


def inverse_or_zero(scale):
    return jnp.where(scale > 0, 1.0 / jnp.where(scale > 0, scale, 1.0), 0.0)


def largest(value):
    return jnp.max(jnp.max(jnp.abs(value), axis=0, keepdims=True), axis=1, keepdims=True)


def split_kernel(*refs):
    count = (len(refs) - 4) // 2
    sources, out_ref = refs[:count], refs[count]
    blocks, out, in_sem, out_sem = refs[count + 1 : 2 * count + 1], *refs[2 * count + 1 :]
    groups, _, lanes = out.shape
    some, rows = groups // PIECES, out.shape[1] // count
    loads, stores = [], []
    for i in range(PIECES):
        at = slice(i * some * lanes, (i + 1) * some * lanes)
        for j in range(count):
            load = pltpu.make_async_copy(
                sources[j].at[:, at], blocks[j].at[:, at], in_sem.at[count * i + j]
            )
            load.start()
            loads.append(load)
    for i in range(PIECES):
        for j in range(count):
            loads[count * i + j].wait()
            for g in range(i * some, (i + 1) * some):
                out[g, j * rows : (j + 1) * rows, :] = blocks[j][:, g * lanes : (g + 1) * lanes]
        at = slice(i * some, (i + 1) * some)
        store = pltpu.make_async_copy(out.at[at], out_ref.at[at], out_sem.at[i])
        store.start()
        stores.append(store)
    for store in stores:
        store.wait()


def beside(left, right):
    return jnp.concatenate([left, right], axis=1)


def first_columns_kernel(own_ref, start_ref, out_ref):
    out_ref[...] = dot(own_ref[...], start_ref[...])


def columns_kernel(other_ref, start_ref, columns_ref, out_ref):
    out_ref[...] = columns_ref[...] + dot(other_ref[...], start_ref[...])


def sum_kernel(in_ref, out_ref, *, rows):
    for at in range(0, rows, SUB):
        tiles = [in_ref[i + at : i + at + SUB, :] for i in range(0, in_ref.shape[0], rows)]
        while len(tiles) > 1:
            tiles = [a + b for a, b in zip(tiles[::2], tiles[1::2])]
        for i in range(0, out_ref.shape[0], rows):
            out_ref[i + at : i + at + SUB, :] = tiles[0]


def across_kernel(own_ref, other_ref, c_ref, x_ref, out_ref, unused_ref):
    c = c_ref[...]
    c = c * inverse_or_zero(largest(c))
    x_ref[...] = dot(c, beside(own_ref[...], other_ref[...]), 0, 0)
    out_ref[...] = c


def image_kernel(own_ref, other_ref, x_ref, out_ref):
    @pl.when(lax.axis_index("core") == 0)
    def _():
        out_ref[...] = dot(beside(own_ref[...], other_ref[...]), x_ref[...], 1, 1)


def second_image_kernel(t_ref, x_ref, image_ref, out_ref):
    core = lax.axis_index("core")

    @pl.when(core == 0)
    def _():
        out_ref[...] = image_ref[...]

    @pl.when(core == 1)
    def _():
        rows = t_ref.shape[1] // 2
        first = t_ref[:, :rows, :].reshape(out_ref.shape)
        second = t_ref[:, rows:, :].reshape(out_ref.shape)
        out_ref[...] = dot(beside(first, second), x_ref[...], 1, 1)


def inverse_factors(matrices):
    size = matrices[0].shape[0]
    blocks = size // SUB
    lane = lax.broadcasted_iota(jnp.int32, (SUB, size), 1)
    sub = lax.broadcasted_iota(jnp.int32, (SUB, size), 0)
    work = [[m[SUB * i : SUB * (i + 1), :] for i in range(blocks)] for m in matrices]

    def columns(rows, low):
        return [
            jnp.broadcast_to(rows[:, low + j : low + j + 1], (SUB, size)) for j in range(SUB)
        ]

    def row(values, j):
        return jnp.broadcast_to(values[j : j + 1, :], (SUB, size))

    for k in range(blocks):
        low = SUB * k
        inside = (lane >= low) & (lane < low + SUB)
        done = []
        for mine in work:
            column = columns(mine[k], low)
            w = jnp.where(inside, (lane == sub + low).astype(jnp.float32), mine[k])
            steps, pivots = [], jnp.ones((SUB, size), jnp.float32)
            for j in range(SUB):
                pivot = row(column[j], j)
                inverse = 1.0 / pivot
                pivots = jnp.where(sub == j, pivot, pivots)
                factor = jnp.where(sub > j, column[j] * inverse, 0.0)
                ahead = {}
                for i in range(j + 1, SUB):
                    ahead[i] = row(column[i], j)
                    column[i] = column[i] - factor * ahead[i]
                reduced = row(w, j)
                w = w - factor * reduced
                steps.append((inverse, ahead, reduced))
            root = lax.rsqrt(pivots)
            root = root * (1.5 - 0.5 * pivots * root * root)
            mine[k] = jnp.where(lane <= sub + low, w * root, 0.0)
            done.append(steps)
        for mine, steps in zip(work, done):
            for i in range(k + 1, blocks):
                column = columns(mine[i], low)
                w = jnp.where(inside, 0.0, mine[i])
                for j, (inverse, ahead, reduced) in enumerate(steps):
                    factor = column[j] * inverse
                    for n in range(j + 1, SUB):
                        column[n] = column[n] - factor * ahead[n]
                    w = w - factor * reduced
                mine[i] = w
    return [jnp.concatenate(mine, axis=0) for mine in work]


def factor_kernel(y_ref, c_ref, out_ref):
    @pl.when(lax.axis_index("core") == 0)
    def _():
        y = y_ref[...]
        scale = largest(y)
        y = y * inverse_or_zero(scale)
        grams = dot(y, beside(y, c_ref[...]), 0, 0)
        lower, lower_w = inverse_factors([grams[:, :LANE], grams[:, LANE:]])
        out_ref[:LANE, :] = lower
        out_ref[LANE : 2 * LANE, :] = lower_w
        out_ref[2 * LANE :, :] = jnp.broadcast_to(scale, (SUB, LANE))


def cross_kernel(own_ref, other_ref, after_ref, out_ref):
    first = lax.axis_index("core") == 0
    y = jnp.where(first, own_ref[...], other_ref[...])
    z = jnp.where(first, other_ref[...], own_ref[...])
    out_ref[...] = dot(y * inverse_or_zero(largest(y)), z, 0, 0)


def final_kernel(own_ref, other_ref, l_ref, l_other_ref, cross_ref, basis_ref, operator_ref):
    first = lax.axis_index("core") == 0
    factors = jnp.where(first, l_ref[...], l_other_ref[...])
    lower, lower_w = factors[:LANE], factors[LANE : 2 * LANE]
    scale = factors[2 * LANE : 2 * LANE + 1]
    rows, total = basis_ref.shape[0], own_ref.shape[0]
    place = lax.axis_index("x") * lax.axis_size("z") + lax.axis_index("z")
    at = pl.ds(pl.multiple_of(place * rows, rows), rows)
    mine = jnp.where(first, own_ref[at, :], other_ref[at, :]) * inverse_or_zero(scale)
    basis_ref[...] = dot(mine * jnp.sqrt(jnp.float32(total)), lower, 1, 1)
    operator_ref[...] = dot(dot(lower, cross_ref[...]), lower_w, 1, 1) * lax.rsqrt(scale)


def exchanged_rows(values, axis):
    count = lax.axis_size(axis)
    return exchanged(values.reshape(count, -1, LANE), axis).reshape(values.shape)


def summed_over_chips(part, name):
    rows = part.shape[0] // lax.axis_size(PLANE)
    kernel = functools.partial(sum_kernel, rows=rows)
    line = (lax.axis_size("z") * rows, LANE)
    (copies,) = call(kernel, name + "_plane", [line], [exchanged_rows(part, PLANE)])
    (copies,) = call(kernel, name + "_line", [part.shape], [exchanged_rows(copies, "z")])
    return exchanged_rows(copies, PLANE)


def split(name, *sources):
    rows, cols = sources[0].shape
    shape = (lax.axis_size(ROWS), len(sources) * rows, LANE)
    scratch = [pltpu.VMEM((rows, cols), jnp.float32)] * len(sources) + [
        pltpu.VMEM(shape, jnp.float32),
        pltpu.SemaphoreType.DMA((len(sources) * PIECES,)),
        pltpu.SemaphoreType.DMA((PIECES,)),
    ]
    return call(split_kernel, name, [shape], sources, scratch, pl.ANY)[0]


def on_device(hankel, shifted, start_basis):
    groups, rows_dev = lax.axis_size(ROWS), hankel.shape[0]
    rows = groups * rows_dev
    start_other = from_other_core(start_basis)
    shifted_other = to_second(shifted)
    pieces, start_other = lax.optimization_barrier((split("split", hankel), start_other))
    own = exchanged(pieces, ROWS).reshape(rows, LANE)
    other = from_other_core(own)
    (c_part,) = call(first_columns_kernel, "first_columns", [(rows, LANE)], [own, start_basis])
    both = (groups, 2 * rows_dev, LANE)

    def project(own, other, c_part, start_other, shifted, shifted_other):
        (c_part,) = call(columns_kernel, "columns", [(rows, LANE)], [other, start_other, c_part])
        c = summed_over_chips(c_part, "columns")
        shapes = [(LANE, 2 * LANE), (rows, LANE), both]
        return tuple(call(across_kernel, "across", shapes, [own, other, c]))

    def relay(own, other, c_part, start_other, shifted, shifted_other):
        t = exchanged(split("split_shifted", shifted_other, shifted), ROWS)
        return jnp.zeros((LANE, 2 * LANE), jnp.float32), jnp.zeros((rows, LANE), jnp.float32), t

    x, c, t = lax.cond(
        lax.axis_index("core") == 0, project, relay,
        own, other, c_part, start_other, shifted, shifted_other,
    )
    x_other = from_other_core(x)
    (part,) = call(image_kernel, "image", [(rows, LANE)], [own, other, x])
    (part,) = call(second_image_kernel, "second_image", [(rows, LANE)], [t, x_other, part])
    part = summed_over_chips(part, "image")
    part_other = from_other_core(part)
    (factors,) = call(factor_kernel, "factors", [(2 * LANE + SUB, LANE)], [part, c])
    (cross,) = call(cross_kernel, "cross", [(LANE, LANE)], [part, part_other, factors])
    return call(
        final_kernel,
        "results",
        [(rows_dev, LANE), (LANE, LANE)],
        [part, part_other, factors, from_other_core(factors), cross],
    )


def solution(mesh):
    finer = Mesh(mesh.devices.reshape(4, 8, 4, 2), ("x", "z", "y", "core"))
    placed = (P(ROWS, COLS), P(ROWS, COLS), P((*COLS, *ROWS), None))

    def whole(*blocks):
        return tuple(on_device(*blocks))

    return jax.shard_map(
        whole, mesh=finer, in_specs=placed, out_specs=(P(ROWS, None), P()), check_vma=False
    )
```

```python
import functools

import jax
import jax.numpy as jnp
from jax import lax
from jax.experimental import pallas as pl
from jax.experimental.pallas import tpu as pltpu
from jax.sharding import Mesh
from jax.sharding import PartitionSpec as P

ROWS = ("x", "z")
COLS = ("y", "core")
PLANE = ("x", "y")
SUB, LANE = 8, 128
PIECES = 4


def exchanged(blocks, axis):
    return lax.all_to_all(blocks, axis, 0, 0, tiled=True)


def from_other_core(value):
    return lax.ppermute(value, "core", [(0, 1), (1, 0)])


def call(kernel, name, shapes, arrays, scratch=(), space=pltpu.VMEM):
    return pl.pallas_call(
        kernel,
        name=name,
        out_shape=[jax.ShapeDtypeStruct(shape, jnp.float32) for shape in shapes],
        in_specs=[pl.BlockSpec(memory_space=space)] * len(arrays),
        out_specs=[pl.BlockSpec(memory_space=space)] * len(shapes),
        scratch_shapes=scratch,
        compiler_params=pltpu.CompilerParams(vmem_limit_bytes=(24 if space is pltpu.VMEM else 60) << 20),
    )(*arrays)


def dot(left, right, left_dim=1, right_dim=0):
    return lax.dot_general(
        left,
        right,
        (((left_dim,), (right_dim,)), ((), ())),
        precision=lax.Precision.HIGHEST,
        preferred_element_type=jnp.float32,
    )


def inverse_or_zero(scale):
    return jnp.where(scale > 0, 1.0 / jnp.where(scale > 0, scale, 1.0), 0.0)


def largest(value):
    return jnp.max(jnp.max(jnp.abs(value), axis=0, keepdims=True), axis=1, keepdims=True)


def split_kernel(*refs):
    count = (len(refs) - 4) // 2
    sources, out_ref = refs[:count], refs[count]
    blocks, out, in_sem, out_sem = refs[count + 1 : 2 * count + 1], *refs[2 * count + 1 :]
    groups, _, lanes = out.shape
    some, rows = groups // PIECES, out.shape[1] // count
    loads, stores = [], []
    for i in range(PIECES):
        at = slice(i * some * lanes, (i + 1) * some * lanes)
        for j in range(count):
            load = pltpu.make_async_copy(
                sources[j].at[:, at], blocks[j].at[:, at], in_sem.at[count * i + j]
            )
            load.start()
            loads.append(load)
    for i in range(PIECES):
        for j in range(count):
            loads[count * i + j].wait()
            for g in range(i * some, (i + 1) * some):
                out[g, j * rows : (j + 1) * rows, :] = blocks[j][:, g * lanes : (g + 1) * lanes]
        at = slice(i * some, (i + 1) * some)
        store = pltpu.make_async_copy(out.at[at], out_ref.at[at], out_sem.at[i])
        store.start()
        stores.append(store)
    for store in stores:
        store.wait()


def beside(left, right):
    return jnp.concatenate([left, right], axis=1)


def first_columns_kernel(own_ref, start_ref, out_ref):
    out_ref[...] = dot(own_ref[...], start_ref[...])


def columns_kernel(other_ref, start_ref, columns_ref, out_ref):
    out_ref[...] = columns_ref[...] + dot(other_ref[...], start_ref[...])


def sum_kernel(in_ref, out_ref, *, rows):
    for at in range(0, rows, SUB):
        tiles = [in_ref[i + at : i + at + SUB, :] for i in range(0, in_ref.shape[0], rows)]
        while len(tiles) > 1:
            tiles = [a + b for a, b in zip(tiles[::2], tiles[1::2])]
        for i in range(0, out_ref.shape[0], rows):
            out_ref[i + at : i + at + SUB, :] = tiles[0]


def across_kernel(own_ref, other_ref, c_ref, x_ref, out_ref, unused_ref):
    c = c_ref[...]
    c = c * inverse_or_zero(largest(c))
    x_ref[...] = dot(c, beside(own_ref[...], other_ref[...]), 0, 0)
    out_ref[...] = c


def image_kernel(own_ref, other_ref, x_ref, out_ref):
    @pl.when(lax.axis_index("core") == 0)
    def _():
        out_ref[...] = dot(beside(own_ref[...], other_ref[...]), x_ref[...], 1, 1)


def second_image_kernel(t_ref, x_ref, image_ref, out_ref):
    core = lax.axis_index("core")

    @pl.when(core == 0)
    def _():
        out_ref[...] = image_ref[...]

    @pl.when(core == 1)
    def _():
        rows = t_ref.shape[1] // 2
        first = t_ref[:, :rows, :].reshape(out_ref.shape)
        second = t_ref[:, rows:, :].reshape(out_ref.shape)
        out_ref[...] = dot(beside(first, second), x_ref[...], 1, 1)


def inverse_factors(matrices):
    size = matrices[0].shape[0]
    blocks = size // SUB
    lane = lax.broadcasted_iota(jnp.int32, (SUB, size), 1)
    sub = lax.broadcasted_iota(jnp.int32, (SUB, size), 0)
    work = [[m[SUB * i : SUB * (i + 1), :] for i in range(blocks)] for m in matrices]

    def columns(rows, low):
        return [
            jnp.broadcast_to(rows[:, low + j : low + j + 1], (SUB, size)) for j in range(SUB)
        ]

    def row(values, j):
        return jnp.broadcast_to(values[j : j + 1, :], (SUB, size))

    for k in range(blocks):
        low = SUB * k
        inside = (lane >= low) & (lane < low + SUB)
        done = []
        for mine in work:
            column = columns(mine[k], low)
            w = jnp.where(inside, (lane == sub + low).astype(jnp.float32), mine[k])
            steps, pivots = [], jnp.ones((SUB, size), jnp.float32)
            for j in range(SUB):
                pivot = row(column[j], j)
                inverse = 1.0 / pivot
                pivots = jnp.where(sub == j, pivot, pivots)
                factor = jnp.where(sub > j, column[j] * inverse, 0.0)
                ahead = {}
                for i in range(j + 1, SUB):
                    ahead[i] = row(column[i], j)
                    column[i] = column[i] - factor * ahead[i]
                reduced = row(w, j)
                w = w - factor * reduced
                steps.append((inverse, ahead, reduced))
            root = lax.rsqrt(pivots)
            root = root * (1.5 - 0.5 * pivots * root * root)
            mine[k] = jnp.where(lane <= sub + low, w * root, 0.0)
            done.append(steps)
        for mine, steps in zip(work, done):
            for i in range(k + 1, blocks):
                column = columns(mine[i], low)
                w = jnp.where(inside, 0.0, mine[i])
                for j, (inverse, ahead, reduced) in enumerate(steps):
                    factor = column[j] * inverse
                    for n in range(j + 1, SUB):
                        column[n] = column[n] - factor * ahead[n]
                    w = w - factor * reduced
                mine[i] = w
    return [jnp.concatenate(mine, axis=0) for mine in work]


def factor_kernel(y_ref, c_ref, out_ref):
    @pl.when(lax.axis_index("core") == 0)
    def _():
        y = y_ref[...]
        scale = largest(y)
        y = y * inverse_or_zero(scale)
        grams = dot(y, beside(y, c_ref[...]), 0, 0)
        lower, lower_w = inverse_factors([grams[:, :LANE], grams[:, LANE:]])
        out_ref[:LANE, :] = lower
        out_ref[LANE : 2 * LANE, :] = lower_w
        out_ref[2 * LANE :, :] = jnp.broadcast_to(scale, (SUB, LANE))


def cross_kernel(own_ref, other_ref, after_ref, out_ref):
    first = lax.axis_index("core") == 0
    y = jnp.where(first, own_ref[...], other_ref[...])
    z = jnp.where(first, other_ref[...], own_ref[...])
    out_ref[...] = dot(y * inverse_or_zero(largest(y)), z, 0, 0)


def final_kernel(own_ref, other_ref, l_ref, l_other_ref, cross_ref, basis_ref, operator_ref):
    first = lax.axis_index("core") == 0
    factors = jnp.where(first, l_ref[...], l_other_ref[...])
    lower, lower_w = factors[:LANE], factors[LANE : 2 * LANE]
    scale = factors[2 * LANE : 2 * LANE + 1]
    rows, total = basis_ref.shape[0], own_ref.shape[0]
    place = lax.axis_index("x") * lax.axis_size("z") + lax.axis_index("z")
    at = pl.ds(pl.multiple_of(place * rows, rows), rows)
    mine = jnp.where(first, own_ref[at, :], other_ref[at, :]) * inverse_or_zero(scale)
    basis_ref[...] = dot(mine * jnp.sqrt(jnp.float32(total)), lower, 1, 1)
    operator_ref[...] = dot(dot(lower, cross_ref[...]), lower_w, 1, 1) * lax.rsqrt(scale)


def exchanged_rows(values, axis):
    count = lax.axis_size(axis)
    return exchanged(values.reshape(count, -1, LANE), axis).reshape(values.shape)


def summed_over_chips(part, name):
    rows = part.shape[0] // lax.axis_size(PLANE)
    kernel = functools.partial(sum_kernel, rows=rows)
    line = (lax.axis_size("z") * rows, LANE)
    (copies,) = call(kernel, name + "_plane", [line], [exchanged_rows(part, PLANE)])
    (copies,) = call(kernel, name + "_line", [part.shape], [exchanged_rows(copies, "z")])
    return exchanged_rows(copies, PLANE)


def split(name, *sources):
    rows, cols = sources[0].shape
    shape = (lax.axis_size(ROWS), len(sources) * rows, LANE)
    scratch = [pltpu.VMEM((rows, cols), jnp.float32)] * len(sources) + [
        pltpu.VMEM(shape, jnp.float32),
        pltpu.SemaphoreType.DMA((len(sources) * PIECES,)),
        pltpu.SemaphoreType.DMA((PIECES,)),
    ]
    return call(split_kernel, name, [shape], sources, scratch, pl.ANY)[0]


def on_device(hankel, shifted, start_basis):
    groups, rows_dev = lax.axis_size(ROWS), hankel.shape[0]
    rows = groups * rows_dev
    start_other = from_other_core(start_basis)
    shifted_other = from_other_core(shifted)
    pieces, start_other, shifted_other = lax.optimization_barrier(
        (split("split", hankel), start_other, shifted_other)
    )
    own = exchanged(pieces, ROWS).reshape(rows, LANE)
    other = from_other_core(own)
    (c_part,) = call(first_columns_kernel, "first_columns", [(rows, LANE)], [own, start_basis])
    both = (groups, 2 * rows_dev, LANE)

    def project(own, other, c_part, start_other, shifted, shifted_other):
        (c_part,) = call(columns_kernel, "columns", [(rows, LANE)], [other, start_other, c_part])
        c = summed_over_chips(c_part, "columns")
        shapes = [(LANE, 2 * LANE), (rows, LANE), both]
        return tuple(call(across_kernel, "across", shapes, [own, other, c]))

    def relay(own, other, c_part, start_other, shifted, shifted_other):
        t = exchanged(split("split_shifted", shifted_other, shifted), ROWS)
        return jnp.zeros((LANE, 2 * LANE), jnp.float32), jnp.zeros((rows, LANE), jnp.float32), t

    x, c, t = lax.cond(
        lax.axis_index("core") == 0, project, relay,
        own, other, c_part, start_other, shifted, shifted_other,
    )
    x_other = from_other_core(x)
    (part,) = call(image_kernel, "image", [(rows, LANE)], [own, other, x])
    (part,) = call(second_image_kernel, "second_image", [(rows, LANE)], [t, x_other, part])
    part = summed_over_chips(part, "image")
    part_other = from_other_core(part)
    (factors,) = call(factor_kernel, "factors", [(2 * LANE + SUB, LANE)], [part, c])
    (cross,) = call(cross_kernel, "cross", [(LANE, LANE)], [part, part_other, factors])
    return call(
        final_kernel,
        "results",
        [(rows_dev, LANE), (LANE, LANE)],
        [part, part_other, factors, from_other_core(factors), cross],
    )


def solution(mesh):
    finer = Mesh(mesh.devices.reshape(4, 8, 4, 2), ("x", "z", "y", "core"))
    placed = (P(ROWS, COLS), P(ROWS, COLS), P((*COLS, *ROWS), None))

    def whole(*blocks):
        return tuple(on_device(*blocks))

    return jax.shard_map(
        whole, mesh=finer, in_specs=placed, out_specs=(P(ROWS, None), P()), check_vma=False
    )
```

```python
import functools

import jax
import jax.numpy as jnp
from jax import lax
from jax.experimental import pallas as pl
from jax.experimental.pallas import tpu as pltpu
from jax.sharding import Mesh
from jax.sharding import PartitionSpec as P

ROWS = ("x", "z")
COLS = ("y", "core")
PLANE = ("x", "y")
SUB, LANE = 8, 128
PIECES = 4


def exchanged(blocks, axis):
    return lax.all_to_all(blocks, axis, 0, 0, tiled=True)


def from_other_core(value):
    return lax.ppermute(value, "core", [(0, 1), (1, 0)])


def call(kernel, name, shapes, arrays, scratch=(), space=pltpu.VMEM):
    return pl.pallas_call(
        kernel,
        name=name,
        out_shape=[jax.ShapeDtypeStruct(shape, jnp.float32) for shape in shapes],
        in_specs=[pl.BlockSpec(memory_space=space)] * len(arrays),
        out_specs=[pl.BlockSpec(memory_space=pltpu.VMEM)] * len(shapes),
        scratch_shapes=scratch,
        compiler_params=pltpu.CompilerParams(vmem_limit_bytes=(24 if space is pltpu.VMEM else 60) << 20),
    )(*arrays)


def dot(left, right, left_dim=1, right_dim=0):
    return lax.dot_general(
        left,
        right,
        (((left_dim,), (right_dim,)), ((), ())),
        precision=lax.Precision.HIGHEST,
        preferred_element_type=jnp.float32,
    )


def inverse_or_zero(scale):
    return jnp.where(scale > 0, 1.0 / jnp.where(scale > 0, scale, 1.0), 0.0)


def largest(value):
    return jnp.max(jnp.max(jnp.abs(value), axis=0, keepdims=True), axis=1, keepdims=True)


def split_kernel(*refs):
    count = (len(refs) - 2) // 2
    sources, out_ref = refs[:count], refs[count]
    blocks, sem = refs[count + 1 : 2 * count + 1], refs[2 * count + 1]
    groups, _, lanes = out_ref.shape
    some, rows = groups // PIECES, out_ref.shape[1] // count
    loads = []
    for i in range(PIECES):
        at = slice(i * some * lanes, (i + 1) * some * lanes)
        for j in range(count):
            load = pltpu.make_async_copy(
                sources[j].at[:, at], blocks[j].at[:, at], sem.at[count * i + j]
            )
            load.start()
            loads.append(load)
    for i in range(PIECES):
        for j in range(count):
            loads[count * i + j].wait()
            for g in range(i * some, (i + 1) * some):
                block = blocks[j][:, g * lanes : (g + 1) * lanes]
                out_ref[g, j * rows : (j + 1) * rows, :] = block


def beside(left, right):
    return jnp.concatenate([left, right], axis=1)


def first_columns_kernel(own_ref, start_ref, out_ref):
    out_ref[...] = dot(own_ref[...], start_ref[...])


def columns_kernel(other_ref, start_ref, columns_ref, out_ref):
    out_ref[...] = columns_ref[...] + dot(other_ref[...], start_ref[...])


def sum_kernel(in_ref, out_ref, *, rows):
    for at in range(0, rows, SUB):
        tiles = [in_ref[i + at : i + at + SUB, :] for i in range(0, in_ref.shape[0], rows)]
        while len(tiles) > 1:
            tiles = [a + b for a, b in zip(tiles[::2], tiles[1::2])]
        for i in range(0, out_ref.shape[0], rows):
            out_ref[i + at : i + at + SUB, :] = tiles[0]


def across_kernel(own_ref, other_ref, c_ref, x_ref, out_ref, unused_ref):
    c = c_ref[...]
    c = c * inverse_or_zero(largest(c))
    x_ref[...] = dot(c, beside(own_ref[...], other_ref[...]), 0, 0)
    out_ref[...] = c


def image_kernel(own_ref, other_ref, x_ref, out_ref):
    @pl.when(lax.axis_index("core") == 0)
    def _():
        out_ref[...] = dot(beside(own_ref[...], other_ref[...]), x_ref[...], 1, 1)


def second_image_kernel(t_ref, x_ref, image_ref, out_ref):
    core = lax.axis_index("core")

    @pl.when(core == 0)
    def _():
        out_ref[...] = image_ref[...]

    @pl.when(core == 1)
    def _():
        rows = t_ref.shape[1] // 2
        first = t_ref[:, :rows, :].reshape(out_ref.shape)
        second = t_ref[:, rows:, :].reshape(out_ref.shape)
        out_ref[...] = dot(beside(first, second), x_ref[...], 1, 1)


def inverse_factors(matrices):
    size = matrices[0].shape[0]
    blocks = size // SUB
    lane = lax.broadcasted_iota(jnp.int32, (SUB, size), 1)
    sub = lax.broadcasted_iota(jnp.int32, (SUB, size), 0)
    work = [[m[SUB * i : SUB * (i + 1), :] for i in range(blocks)] for m in matrices]

    def columns(rows, low):
        return [
            jnp.broadcast_to(rows[:, low + j : low + j + 1], (SUB, size)) for j in range(SUB)
        ]

    def row(values, j):
        return jnp.broadcast_to(values[j : j + 1, :], (SUB, size))

    for k in range(blocks):
        low = SUB * k
        inside = (lane >= low) & (lane < low + SUB)
        done = []
        for mine in work:
            column = columns(mine[k], low)
            w = jnp.where(inside, (lane == sub + low).astype(jnp.float32), mine[k])
            steps, pivots = [], jnp.ones((SUB, size), jnp.float32)
            for j in range(SUB):
                pivot = row(column[j], j)
                inverse = 1.0 / pivot
                pivots = jnp.where(sub == j, pivot, pivots)
                factor = jnp.where(sub > j, column[j] * inverse, 0.0)
                ahead = {}
                for i in range(j + 1, SUB):
                    ahead[i] = row(column[i], j)
                    column[i] = column[i] - factor * ahead[i]
                reduced = row(w, j)
                w = w - factor * reduced
                steps.append((inverse, ahead, reduced))
            root = lax.rsqrt(pivots)
            root = root * (1.5 - 0.5 * pivots * root * root)
            mine[k] = jnp.where(lane <= sub + low, w * root, 0.0)
            done.append(steps)
        for mine, steps in zip(work, done):
            for i in range(k + 1, blocks):
                column = columns(mine[i], low)
                w = jnp.where(inside, 0.0, mine[i])
                for j, (inverse, ahead, reduced) in enumerate(steps):
                    factor = column[j] * inverse
                    for n in range(j + 1, SUB):
                        column[n] = column[n] - factor * ahead[n]
                    w = w - factor * reduced
                mine[i] = w
    return [jnp.concatenate(mine, axis=0) for mine in work]


def factor_kernel(y_ref, c_ref, out_ref):
    @pl.when(lax.axis_index("core") == 0)
    def _():
        y = y_ref[...]
        scale = largest(y)
        y = y * inverse_or_zero(scale)
        grams = dot(y, beside(y, c_ref[...]), 0, 0)
        lower, lower_w = inverse_factors([grams[:, :LANE], grams[:, LANE:]])
        out_ref[:LANE, :] = lower
        out_ref[LANE : 2 * LANE, :] = lower_w
        out_ref[2 * LANE :, :] = jnp.broadcast_to(scale, (SUB, LANE))


def cross_kernel(own_ref, other_ref, after_ref, out_ref):
    first = lax.axis_index("core") == 0
    y = jnp.where(first, own_ref[...], other_ref[...])
    z = jnp.where(first, other_ref[...], own_ref[...])
    out_ref[...] = dot(y * inverse_or_zero(largest(y)), z, 0, 0)


def final_kernel(own_ref, other_ref, l_ref, l_other_ref, cross_ref, basis_ref, operator_ref):
    first = lax.axis_index("core") == 0
    factors = jnp.where(first, l_ref[...], l_other_ref[...])
    lower, lower_w = factors[:LANE], factors[LANE : 2 * LANE]
    scale = factors[2 * LANE : 2 * LANE + 1]
    rows, total = basis_ref.shape[0], own_ref.shape[0]
    place = lax.axis_index("x") * lax.axis_size("z") + lax.axis_index("z")
    at = pl.ds(pl.multiple_of(place * rows, rows), rows)
    mine = jnp.where(first, own_ref[at, :], other_ref[at, :]) * inverse_or_zero(scale)
    basis_ref[...] = dot(mine * jnp.sqrt(jnp.float32(total)), lower, 1, 1)
    operator_ref[...] = dot(dot(lower, cross_ref[...]), lower_w, 1, 1) * lax.rsqrt(scale)


def exchanged_rows(values, axis):
    count = lax.axis_size(axis)
    return exchanged(values.reshape(count, -1, LANE), axis).reshape(values.shape)


def summed_over_chips(part, name):
    rows = part.shape[0] // lax.axis_size(PLANE)
    kernel = functools.partial(sum_kernel, rows=rows)
    line = (lax.axis_size("z") * rows, LANE)
    (copies,) = call(kernel, name + "_plane", [line], [exchanged_rows(part, PLANE)])
    (copies,) = call(kernel, name + "_line", [part.shape], [exchanged_rows(copies, "z")])
    return exchanged_rows(copies, PLANE)


def split(name, *sources):
    rows, cols = sources[0].shape
    shape = (lax.axis_size(ROWS), len(sources) * rows, LANE)
    scratch = [pltpu.VMEM((rows, cols), jnp.float32)] * len(sources) + [
        pltpu.SemaphoreType.DMA((len(sources) * PIECES,)),
    ]
    return call(split_kernel, name, [shape], sources, scratch, pl.ANY)[0]


def on_device(hankel, shifted, start_basis):
    groups, rows_dev = lax.axis_size(ROWS), hankel.shape[0]
    rows = groups * rows_dev
    start_other = from_other_core(start_basis)
    shifted_other = from_other_core(shifted)
    pieces, start_other, shifted_other = lax.optimization_barrier(
        (split("split", hankel), start_other, shifted_other)
    )
    own = exchanged(pieces, ROWS).reshape(rows, LANE)
    other = from_other_core(own)
    (c_part,) = call(first_columns_kernel, "first_columns", [(rows, LANE)], [own, start_basis])
    both = (groups, 2 * rows_dev, LANE)

    def project(own, other, c_part, start_other, shifted, shifted_other):
        (c_part,) = call(columns_kernel, "columns", [(rows, LANE)], [other, start_other, c_part])
        c = summed_over_chips(c_part, "columns")
        shapes = [(LANE, 2 * LANE), (rows, LANE), both]
        return tuple(call(across_kernel, "across", shapes, [own, other, c]))

    def relay(own, other, c_part, start_other, shifted, shifted_other):
        t = exchanged(split("split_shifted", shifted_other, shifted), ROWS)
        return jnp.zeros((LANE, 2 * LANE), jnp.float32), jnp.zeros((rows, LANE), jnp.float32), t

    x, c, t = lax.cond(
        lax.axis_index("core") == 0, project, relay,
        own, other, c_part, start_other, shifted, shifted_other,
    )
    x_other = from_other_core(x)
    (part,) = call(image_kernel, "image", [(rows, LANE)], [own, other, x])
    (part,) = call(second_image_kernel, "second_image", [(rows, LANE)], [t, x_other, part])
    part = summed_over_chips(part, "image")
    part_other = from_other_core(part)
    (factors,) = call(factor_kernel, "factors", [(2 * LANE + SUB, LANE)], [part, c])
    (cross,) = call(cross_kernel, "cross", [(LANE, LANE)], [part, part_other, factors])
    return call(
        final_kernel,
        "results",
        [(rows_dev, LANE), (LANE, LANE)],
        [part, part_other, factors, from_other_core(factors), cross],
    )


def solution(mesh):
    finer = Mesh(mesh.devices.reshape(4, 8, 4, 2), ("x", "z", "y", "core"))
    placed = (P(ROWS, COLS), P(ROWS, COLS), P((*COLS, *ROWS), None))

    def whole(*blocks):
        return tuple(on_device(*blocks))

    return jax.shard_map(
        whole, mesh=finer, in_specs=placed, out_specs=(P(ROWS, None), P()), check_vma=False
    )
```

```python
import functools

import jax
import jax.numpy as jnp
from jax import lax
from jax.experimental import pallas as pl
from jax.experimental.pallas import tpu as pltpu
from jax.sharding import Mesh
from jax.sharding import PartitionSpec as P

ROWS = ("x", "z")
COLS = ("y", "core")
PLANE = ("x", "y")
SUB, LANE = 8, 128
PIECES = 8


def exchanged(blocks, axis):
    return lax.all_to_all(blocks, axis, 0, 0, tiled=True)


def from_other_core(value):
    return lax.ppermute(value, "core", [(0, 1), (1, 0)])


def call(kernel, name, shapes, arrays, scratch=(), space=pltpu.VMEM):
    return pl.pallas_call(
        kernel,
        name=name,
        out_shape=[jax.ShapeDtypeStruct(shape, jnp.float32) for shape in shapes],
        in_specs=[pl.BlockSpec(memory_space=space)] * len(arrays),
        out_specs=[pl.BlockSpec(memory_space=space)] * len(shapes),
        scratch_shapes=scratch,
        compiler_params=pltpu.CompilerParams(vmem_limit_bytes=(24 if space is pltpu.VMEM else 60) << 20),
    )(*arrays)


def dot(left, right, left_dim=1, right_dim=0):
    return lax.dot_general(
        left,
        right,
        (((left_dim,), (right_dim,)), ((), ())),
        precision=lax.Precision.HIGHEST,
        preferred_element_type=jnp.float32,
    )


def inverse_or_zero(scale):
    return jnp.where(scale > 0, 1.0 / jnp.where(scale > 0, scale, 1.0), 0.0)


def largest(value):
    return jnp.max(jnp.max(jnp.abs(value), axis=0, keepdims=True), axis=1, keepdims=True)


def split_kernel(*refs):
    count = (len(refs) - 4) // 2
    sources, out_ref = refs[:count], refs[count]
    blocks, out, in_sem, out_sem = refs[count + 1 : 2 * count + 1], *refs[2 * count + 1 :]
    groups, _, lanes = out.shape
    some, rows = groups // PIECES, out.shape[1] // count
    loads, stores = [], []
    for i in range(PIECES):
        at = slice(i * some * lanes, (i + 1) * some * lanes)
        for j in range(count):
            load = pltpu.make_async_copy(
                sources[j].at[:, at], blocks[j].at[:, at], in_sem.at[count * i + j]
            )
            load.start()
            loads.append(load)
    for i in range(PIECES):
        for j in range(count):
            loads[count * i + j].wait()
            for g in range(i * some, (i + 1) * some):
                out[g, j * rows : (j + 1) * rows, :] = blocks[j][:, g * lanes : (g + 1) * lanes]
        at = slice(i * some, (i + 1) * some)
        store = pltpu.make_async_copy(out.at[at], out_ref.at[at], out_sem.at[i])
        store.start()
        stores.append(store)
    for store in stores:
        store.wait()


def beside(left, right):
    return jnp.concatenate([left, right], axis=1)


def first_columns_kernel(own_ref, start_ref, out_ref):
    out_ref[...] = dot(own_ref[...], start_ref[...])


def columns_kernel(other_ref, start_ref, columns_ref, out_ref):
    out_ref[...] = columns_ref[...] + dot(other_ref[...], start_ref[...])


def sum_kernel(in_ref, out_ref, *, rows):
    for at in range(0, rows, SUB):
        tiles = [in_ref[i + at : i + at + SUB, :] for i in range(0, in_ref.shape[0], rows)]
        while len(tiles) > 1:
            tiles = [a + b for a, b in zip(tiles[::2], tiles[1::2])]
        for i in range(0, out_ref.shape[0], rows):
            out_ref[i + at : i + at + SUB, :] = tiles[0]


def across_kernel(own_ref, other_ref, c_ref, x_ref, out_ref, unused_ref):
    c = c_ref[...]
    c = c * inverse_or_zero(largest(c))
    x_ref[...] = dot(c, beside(own_ref[...], other_ref[...]), 0, 0)
    out_ref[...] = c


def image_kernel(own_ref, other_ref, x_ref, out_ref):
    @pl.when(lax.axis_index("core") == 0)
    def _():
        out_ref[...] = dot(beside(own_ref[...], other_ref[...]), x_ref[...], 1, 1)


def second_image_kernel(t_ref, x_ref, image_ref, out_ref):
    core = lax.axis_index("core")

    @pl.when(core == 0)
    def _():
        out_ref[...] = image_ref[...]

    @pl.when(core == 1)
    def _():
        rows = t_ref.shape[1] // 2
        first = t_ref[:, :rows, :].reshape(out_ref.shape)
        second = t_ref[:, rows:, :].reshape(out_ref.shape)
        out_ref[...] = dot(beside(first, second), x_ref[...], 1, 1)


def inverse_factors(matrices):
    size = matrices[0].shape[0]
    blocks = size // SUB
    lane = lax.broadcasted_iota(jnp.int32, (SUB, size), 1)
    sub = lax.broadcasted_iota(jnp.int32, (SUB, size), 0)
    work = [[m[SUB * i : SUB * (i + 1), :] for i in range(blocks)] for m in matrices]

    def columns(rows, low):
        return [
            jnp.broadcast_to(rows[:, low + j : low + j + 1], (SUB, size)) for j in range(SUB)
        ]

    def row(values, j):
        return jnp.broadcast_to(values[j : j + 1, :], (SUB, size))

    for k in range(blocks):
        low = SUB * k
        inside = (lane >= low) & (lane < low + SUB)
        done = []
        for mine in work:
            column = columns(mine[k], low)
            w = jnp.where(inside, (lane == sub + low).astype(jnp.float32), mine[k])
            steps, pivots = [], jnp.ones((SUB, size), jnp.float32)
            for j in range(SUB):
                pivot = row(column[j], j)
                inverse = 1.0 / pivot
                pivots = jnp.where(sub == j, pivot, pivots)
                factor = jnp.where(sub > j, column[j] * inverse, 0.0)
                ahead = {}
                for i in range(j + 1, SUB):
                    ahead[i] = row(column[i], j)
                    column[i] = column[i] - factor * ahead[i]
                reduced = row(w, j)
                w = w - factor * reduced
                steps.append((inverse, ahead, reduced))
            root = lax.rsqrt(pivots)
            root = root * (1.5 - 0.5 * pivots * root * root)
            mine[k] = jnp.where(lane <= sub + low, w * root, 0.0)
            done.append(steps)
        for mine, steps in zip(work, done):
            for i in range(k + 1, blocks):
                column = columns(mine[i], low)
                w = jnp.where(inside, 0.0, mine[i])
                for j, (inverse, ahead, reduced) in enumerate(steps):
                    factor = column[j] * inverse
                    for n in range(j + 1, SUB):
                        column[n] = column[n] - factor * ahead[n]
                    w = w - factor * reduced
                mine[i] = w
    return [jnp.concatenate(mine, axis=0) for mine in work]


def factor_kernel(y_ref, c_ref, out_ref):
    @pl.when(lax.axis_index("core") == 0)
    def _():
        y = y_ref[...]
        scale = largest(y)
        y = y * inverse_or_zero(scale)
        grams = dot(y, beside(y, c_ref[...]), 0, 0)
        lower, lower_w = inverse_factors([grams[:, :LANE], grams[:, LANE:]])
        out_ref[:LANE, :] = lower
        out_ref[LANE : 2 * LANE, :] = lower_w
        out_ref[2 * LANE :, :] = jnp.broadcast_to(scale, (SUB, LANE))


def cross_kernel(own_ref, other_ref, after_ref, out_ref):
    first = lax.axis_index("core") == 0
    y = jnp.where(first, own_ref[...], other_ref[...])
    z = jnp.where(first, other_ref[...], own_ref[...])
    out_ref[...] = dot(y * inverse_or_zero(largest(y)), z, 0, 0)


def final_kernel(own_ref, other_ref, l_ref, l_other_ref, cross_ref, basis_ref, operator_ref):
    first = lax.axis_index("core") == 0
    factors = jnp.where(first, l_ref[...], l_other_ref[...])
    lower, lower_w = factors[:LANE], factors[LANE : 2 * LANE]
    scale = factors[2 * LANE : 2 * LANE + 1]
    rows, total = basis_ref.shape[0], own_ref.shape[0]
    place = lax.axis_index("x") * lax.axis_size("z") + lax.axis_index("z")
    at = pl.ds(pl.multiple_of(place * rows, rows), rows)
    mine = jnp.where(first, own_ref[at, :], other_ref[at, :]) * inverse_or_zero(scale)
    basis_ref[...] = dot(mine * jnp.sqrt(jnp.float32(total)), lower, 1, 1)
    operator_ref[...] = dot(dot(lower, cross_ref[...]), lower_w, 1, 1) * lax.rsqrt(scale)


def exchanged_rows(values, axis):
    count = lax.axis_size(axis)
    return exchanged(values.reshape(count, -1, LANE), axis).reshape(values.shape)


def summed_over_chips(part, name):
    rows = part.shape[0] // lax.axis_size(PLANE)
    kernel = functools.partial(sum_kernel, rows=rows)
    line = (lax.axis_size("z") * rows, LANE)
    (copies,) = call(kernel, name + "_plane", [line], [exchanged_rows(part, PLANE)])
    (copies,) = call(kernel, name + "_line", [part.shape], [exchanged_rows(copies, "z")])
    return exchanged_rows(copies, PLANE)


def split(name, *sources):
    rows, cols = sources[0].shape
    shape = (lax.axis_size(ROWS), len(sources) * rows, LANE)
    scratch = [pltpu.VMEM((rows, cols), jnp.float32)] * len(sources) + [
        pltpu.VMEM(shape, jnp.float32),
        pltpu.SemaphoreType.DMA((len(sources) * PIECES,)),
        pltpu.SemaphoreType.DMA((PIECES,)),
    ]
    return call(split_kernel, name, [shape], sources, scratch, pl.ANY)[0]


def on_device(hankel, shifted, start_basis):
    groups, rows_dev = lax.axis_size(ROWS), hankel.shape[0]
    rows = groups * rows_dev
    start_other = from_other_core(start_basis)
    shifted_other = from_other_core(shifted)
    pieces, start_other, shifted_other = lax.optimization_barrier(
        (split("split", hankel), start_other, shifted_other)
    )
    own = exchanged(pieces, ROWS).reshape(rows, LANE)
    other = from_other_core(own)
    (c_part,) = call(first_columns_kernel, "first_columns", [(rows, LANE)], [own, start_basis])
    both = (groups, 2 * rows_dev, LANE)

    def project(own, other, c_part, start_other, shifted, shifted_other):
        (c_part,) = call(columns_kernel, "columns", [(rows, LANE)], [other, start_other, c_part])
        c = summed_over_chips(c_part, "columns")
        shapes = [(LANE, 2 * LANE), (rows, LANE), both]
        return tuple(call(across_kernel, "across", shapes, [own, other, c]))

    def relay(own, other, c_part, start_other, shifted, shifted_other):
        t = exchanged(split("split_shifted", shifted_other, shifted), ROWS)
        return jnp.zeros((LANE, 2 * LANE), jnp.float32), jnp.zeros((rows, LANE), jnp.float32), t

    x, c, t = lax.cond(
        lax.axis_index("core") == 0, project, relay,
        own, other, c_part, start_other, shifted, shifted_other,
    )
    x_other = from_other_core(x)
    (part,) = call(image_kernel, "image", [(rows, LANE)], [own, other, x])
    (part,) = call(second_image_kernel, "second_image", [(rows, LANE)], [t, x_other, part])
    part = summed_over_chips(part, "image")
    part_other = from_other_core(part)
    (factors,) = call(factor_kernel, "factors", [(2 * LANE + SUB, LANE)], [part, c])
    (cross,) = call(cross_kernel, "cross", [(LANE, LANE)], [part, part_other, factors])
    return call(
        final_kernel,
        "results",
        [(rows_dev, LANE), (LANE, LANE)],
        [part, part_other, factors, from_other_core(factors), cross],
    )


def solution(mesh):
    finer = Mesh(mesh.devices.reshape(4, 8, 4, 2), ("x", "z", "y", "core"))
    placed = (P(ROWS, COLS), P(ROWS, COLS), P((*COLS, *ROWS), None))

    def whole(*blocks):
        return tuple(on_device(*blocks))

    return jax.shard_map(
        whole, mesh=finer, in_specs=placed, out_specs=(P(ROWS, None), P()), check_vma=False
    )
```
